256 devices in a mesh: leaf: 32 (over z, y), front: 8 (over x, core).
Axes of the slice: x: 4, y: 4, z: 8, core: 2. Of those that a mesh axis runs over, the one named last changes fastest.
Arguments:
- section_updates: bfloat16 [32768, 256], P(('leaf', 'front')), may hold values from -6 to 6
- upper_rhs: float32 [126976, 256], P(('leaf', 'front')), may hold values from -6 to 6
- pivot_inverse: bfloat16 [126976, 4096], P('leaf', 'front'), may hold values from -0.09375 to 0.09375
- coupling: bfloat16 [1024, 122880], P('front', 'leaf'), may hold values from -0.09375 to 0.09375
- extend_lists: int32 [62, 8], replicated, may hold values from 0 to 39, as said below
Outputs:
- solution: float32 [126976, 256], P(('leaf', 'front'))
- interface: bfloat16 [32768, 256], P(('leaf', 'front'))
The draws below stay inside these ranges and needn't reach their ends.
Inputs may be any that keep to these rules, and one draw needn't show every extreme that they name: `extend_lists`: each row names 8 different blocks of the parent's frame; the rows of the root's two children name pivot blocks only, below 32.
All inputs are finite; a program needn't handle non-finite values.
Results may differ from the reference program's by a relative error of at most 0.022.
Values may be sent and summed in bfloat16 or wider, within the bound.
A program may use at most 64 MiB of HBM per device.

```python
import jax
import jax.numpy as jnp
from jax import lax

PIV = 4096
UPD = 1024
BLK = 128
RHS = 256
LEVELS = 5
UB = 8
PB = 40
CHILDREN = 62
N_LEAF = 32
N_FRONT = 8


def draw_extend_lists(key, part):
    row_keys = jax.random.split(jax.random.fold_in(key, 11), CHILDREN)
    everywhere = jax.vmap(lambda row_key: jax.random.permutation(row_key, PB)[:UB])(row_keys)
    pivots_only = jax.vmap(lambda row_key: jax.random.permutation(jax.random.fold_in(row_key, 3), PIV // BLK)[:UB])(row_keys)
    first_row = everywhere[0]
    has_last = jnp.any(first_row == PB - 1)
    first_row = first_row.at[0].set(jnp.where(has_last, first_row[0], PB - 1))
    second_row = everywhere[1]
    has_zero = jnp.any(second_row == 0)
    second_row = second_row.at[0].set(jnp.where(has_zero, second_row[0], 0))
    everywhere = everywhere.at[0].set(first_row).at[1].set(second_row)
    near_root = (jnp.arange(CHILDREN) >= CHILDREN - 2)[:, None]
    return jnp.where(near_root, pivots_only, everywhere).astype(jnp.int32)


def level_of(stream_key, dims, pieces, low, top_value):
    level, own = 1.0, jax.random.fold_in(stream_key, 6)
    for position, blocks in pieces:
        steps = jnp.exp(jax.random.uniform(jax.random.fold_in(own, position), (blocks,), jnp.float32, low / len(pieces), top_value / len(pieces)))
        level = level * jnp.repeat(steps, dims[position] // blocks).reshape([-1 if axis == position else 1 for axis in range(len(dims))])
    return level


def centred(rng, extent, deviation, reach, cuts=(), kind=jnp.bfloat16):
    result = jax.random.normal(rng, extent, jnp.float32) * deviation
    if len(cuts) > 0:
        result = level_of(rng, extent, cuts, -0.22, 0.18) * result
    return jnp.clip(result, min=-reach, max=reach).astype(kind)


def setup_inputs(seed: int = 0) -> dict:
    key_list = jax.random.split(jax.random.key(seed), 6)
    section_updates = centred(key_list[0], (N_LEAF * UPD, RHS), 1.0, 6.0, ((0, 256),))
    upper_rhs = centred(key_list[1], ((N_LEAF - 1) * PIV, RHS), 1.0, 6.0, ((0, 256),), jnp.float32)
    pivot_inverse = centred(key_list[2], ((N_LEAF - 1) * PIV, PIV), PIV ** -0.5, 0.09375, ((0, 32), (1, 8)))
    coupling = centred(key_list[3], (UPD, (N_LEAF - 2) * PIV), PIV ** -0.5, 0.09375, ((0, 8), (1, 32)))
    extend_lists = draw_extend_lists(jax.random.fold_in(key_list[5], 71), 0)
    return {"section_updates": section_updates, "upper_rhs": upper_rhs, "pivot_inverse": pivot_inverse, "coupling": coupling, "extend_lists": extend_lists}


def map_products(left, right):
    return lax.map(lambda pair: jnp.dot(pair[0], pair[1], preferred_element_type=jnp.float32), (left, right))


def map_transposed(left, right):
    return lax.map(lambda pair: jnp.dot(pair[0].T, pair[1], preferred_element_type=jnp.float32), (left, right))


def reference(section_updates, upper_rhs, pivot_inverse, coupling, extend_lists):
    band_pivot = PIV - PIV // N_LEAF
    band_couple = PIV - 2 * (PIV // N_LEAF)
    rows_front = PIV // N_FRONT
    band_rhs = rows_front - rows_front // N_LEAF
    inverse_all = pivot_inverse.reshape(N_LEAF, band_pivot, PIV)
    couple_all = coupling.reshape(UPD, N_LEAF, band_couple)
    rhs_all = upper_rhs.reshape(N_LEAF, N_FRONT, band_rhs, RHS)
    updates = section_updates.reshape(N_LEAF, UPD, RHS)
    block_ids = jnp.arange(PB, dtype=jnp.int32)
    child_start = 0
    kept = []
    for height in range(1, LEVELS + 1):
        group_size = 2 ** height
        fronts_here = N_LEAF // group_size
        span_rows = PIV // group_size
        band_start = PIV - PIV // 2 ** (height - 1)
        rhs_len = rows_front // group_size
        rhs_start = rows_front - rows_front // 2 ** (height - 1)
        child_lists = extend_lists[child_start:child_start + 2 * fronts_here]
        onehot = (child_lists[:, :, None] == block_ids[None, None, :]).astype(jnp.float32)
        blocks = updates.astype(jnp.float32).reshape(2 * fronts_here, UB, BLK * RHS)
        placed = jnp.einsum("cjq,cjx->cqx", onehot, blocks, precision=lax.Precision.HIGHEST)
        assembled = placed.reshape(fronts_here, 2, PB * BLK, RHS).sum(axis=1)
        own_rhs = rhs_all[:, :, rhs_start:rhs_start + rhs_len, :]
        own_rhs = own_rhs.reshape(fronts_here, group_size, N_FRONT, rhs_len, RHS).transpose(0, 2, 1, 3, 4).reshape(fronts_here, PIV, RHS)
        rows_half = (own_rhs + assembled[:, :PIV]).astype(jnp.bfloat16)
        inverse_level = inverse_all[:, band_start:band_start + span_rows, :].reshape(fronts_here, PIV, PIV)
        pivot_solve = map_products(inverse_level, rows_half)
        pivot_half = pivot_solve.astype(jnp.bfloat16)
        couple_level = None
        if height < LEVELS:
            couple_level = couple_all[:, :, band_start:band_start + span_rows]
            couple_level = couple_level.reshape(UPD, fronts_here, group_size, span_rows).transpose(1, 0, 2, 3).reshape(fronts_here, UPD, PIV)
            updates = (assembled[:, PIV:] - map_products(couple_level, pivot_half)).astype(jnp.bfloat16)
        kept.append((inverse_level, couple_level, pivot_solve))
        child_start = child_start + 2 * fronts_here
    from_above = None
    packed = []
    for height in range(LEVELS, 0, -1):
        group_size = 2 ** height
        fronts_here = N_LEAF // group_size
        rhs_len = rows_front // group_size
        inverse_level, couple_level, pivot_solve = kept[height - 1]
        if height < LEVELS:
            weight_half = (pivot_solve - map_transposed(couple_level, from_above)).astype(jnp.bfloat16)
            upper_rows = from_above
        else:
            weight_half = pivot_solve.astype(jnp.bfloat16)
            upper_rows = jnp.zeros((fronts_here, UPD, RHS), jnp.bfloat16)
        solved = map_transposed(inverse_level, weight_half)
        packed.append(solved.reshape(fronts_here, N_FRONT, group_size, rhs_len, RHS).transpose(0, 2, 1, 3, 4).reshape(N_LEAF, N_FRONT, rhs_len, RHS))
        frame_half = jnp.concatenate([solved.astype(jnp.bfloat16), upper_rows], axis=1).reshape(fronts_here, PB, BLK * RHS)
        base_row = sum(N_LEAF // 2 ** depth for depth in range(height - 1))
        child_lists = extend_lists[base_row:base_row + 2 * fronts_here]
        parents = jnp.arange(2 * fronts_here, dtype=jnp.int32) // 2
        from_above = frame_half[parents[:, None], child_lists].reshape(2 * fronts_here, UPD, RHS)
    solution = jnp.concatenate(packed[::-1], axis=2).reshape((N_LEAF - 1) * PIV, RHS)
    return solution, from_above.reshape(N_LEAF * UPD, RHS)
```

```python
import jax
import jax.numpy as jnp
from jax import lax
from jax.sharding import PartitionSpec as P

PIV = 4096
UPD = 1024
BLK = 128


def partner(block, axis, stride):
    count = lax.axis_size(axis)
    route = []
    for low in range(count):
        high = low | 1 << stride
        if high != low and high < count:
            route += [(low, high), (high, low)]
    return lax.ppermute(block, axis, route)


def child_base(leaves, height):
    total_rows = 0
    for depth in range(height - 1):
        total_rows = total_rows + leaves // 2**depth
    return total_rows


def list_row(extend_lists, row_index):
    return lax.dynamic_slice_in_dim(extend_lists, row_index, 1, 0)[0]


def upper_bit(position, bit_index):
    return position >> bit_index & 1 == 1


def joined(position, bit_index, portion, partner_rows):
    return jnp.where(
        upper_bit(position, bit_index),
        jnp.concatenate([partner_rows, portion], 0),
        jnp.concatenate([portion, partner_rows], 0),
    )


def gather_own(portion, height, position):
    for bit_index in range(height):
        partner_rows = partner(portion.astype(jnp.bfloat16), "leaf", bit_index).astype(
            portion.dtype
        )
        portion = joined(position, bit_index, portion, partner_rows)
    return portion


def sum_updates(summand, height):
    for bit_index in range(height):
        summand = summand + partner(summand.astype(jnp.bfloat16), "leaf", bit_index).astype(
            summand.dtype
        )
    return summand


def sum_solution(summand, height):
    for bit_index in range(height):
        summand = summand + partner(summand.astype(jnp.bfloat16), "leaf", bit_index).astype(
            summand.dtype
        )
    return summand


def front_sum(summand):
    bits = lax.axis_size("front").bit_length() - 1
    for bit_index in range(bits):
        half = summand.astype(jnp.bfloat16)
        summand = half.astype(jnp.float32) + partner(half, "front", bit_index).astype(
            jnp.float32
        )
    return summand


def per_device(section_updates, upper_rhs, pivot_inverse, coupling, extend_lists):
    leaves = lax.axis_size("leaf")
    fronts = lax.axis_size("front")
    levels = leaves.bit_length() - 1
    position = lax.axis_index("leaf")
    column = lax.axis_index("front")
    rhs_width = upper_rhs.shape[1]
    piv_dev = PIV // fronts
    upd_dev = UPD // fronts
    piv_blocks = piv_dev // BLK
    upd_blocks = upd_dev // BLK
    block_count = UPD // BLK
    local_blocks = jnp.concatenate(
        [
            column * piv_blocks + jnp.arange(piv_blocks, dtype=jnp.int32),
            PIV // BLK + column * upd_blocks + jnp.arange(upd_blocks, dtype=jnp.int32),
        ]
    )
    local_count = piv_blocks + upd_blocks
    carried = section_updates
    saved_part = []
    saved_half = []
    for height in range(1, levels + 1):
        group_size = 2**height
        span_rows = PIV // group_size
        band_start = PIV - PIV // 2 ** (height - 1)
        rhs_len = piv_dev // group_size
        rhs_start = piv_dev - piv_dev // 2 ** (height - 1)
        member = position & group_size - 1
        own_child = child_base(leaves, height) + (position >> height - 1)
        sibling = partner(carried, "leaf", height - 1)
        pair_blocks = lax.all_gather(jnp.stack([carried, sibling]), "front", axis=1, tiled=True)
        pair_lists = jnp.stack(
            [list_row(extend_lists, own_child), list_row(extend_lists, own_child ^ 1)]
        )
        chooser = (pair_lists.reshape(2 * block_count)[None, :] == local_blocks[:, None]).astype(
            jnp.bfloat16
        )
        assembled = jnp.dot(
            chooser,
            pair_blocks.reshape(2 * block_count, BLK * rhs_width),
            preferred_element_type=jnp.float32,
        ).reshape(local_count * BLK, rhs_width)
        own_rows = gather_own(upper_rhs[rhs_start : rhs_start + rhs_len], height, position)
        rows_half = (own_rows + assembled[:piv_dev]).astype(jnp.bfloat16)
        g_share = pivot_inverse[band_start : band_start + span_rows]
        pivot_part = front_sum(
            jnp.dot(g_share, rows_half, preferred_element_type=jnp.float32)
        )
        pivot_half = pivot_part.astype(jnp.bfloat16)
        saved_part.append(pivot_part)
        saved_half.append(pivot_half)
        if height < levels:
            c_share = coupling[:, band_start : band_start + span_rows]
            summand = jnp.dot(c_share, pivot_half, preferred_element_type=jnp.float32)
            frame_upd = assembled[piv_dev:]
            carried = (frame_upd - sum_updates(summand, height)).astype(jnp.bfloat16)
    from_above = carried
    outputs = []
    for height in range(levels, 0, -1):
        group_size = 2**height
        span_rows = PIV // group_size
        band_start = PIV - PIV // 2 ** (height - 1)
        member = position & group_size - 1
        pivot_part = saved_part[height - 1]
        if height < levels:
            c_share = coupling[:, band_start : band_start + span_rows]
            back_total = front_sum(
                jnp.einsum("up,ur->pr", c_share, from_above, preferred_element_type=jnp.float32)
            )
            weight_half = (pivot_part - back_total).astype(jnp.bfloat16)
            upper_rows = from_above
        else:
            weight_half = saved_half[height - 1]
            upper_rows = jnp.zeros((upd_dev, rhs_width), jnp.bfloat16)
        g_share = pivot_inverse[band_start : band_start + span_rows]
        solve_term = jnp.einsum(
            "cp,cr->pr", g_share, weight_half, preferred_element_type=jnp.float32
        )
        part_len = piv_dev // group_size
        summed = sum_solution(solve_term, height)
        portion = lax.dynamic_slice_in_dim(summed, member * part_len, part_len, 0)
        rows_half = summed.astype(jnp.bfloat16)
        outputs.append(portion)
        frame_half = jnp.concatenate([rows_half, upper_rows], 0).reshape(
            local_count, BLK * rhs_width
        )
        child_list = list_row(extend_lists, child_base(leaves, height) + (position >> height - 1))
        picker = (child_list[:, None] == local_blocks[None, :]).astype(jnp.bfloat16)
        outgoing = (
            jnp.dot(picker, frame_half, preferred_element_type=jnp.float32)
            .astype(jnp.bfloat16)
            .reshape(fronts, upd_dev, rhs_width)
        )
        incoming = lax.all_to_all(outgoing, "front", split_axis=0, concat_axis=0, tiled=True)
        from_above = jnp.sum(incoming, axis=0, dtype=jnp.float32).astype(jnp.bfloat16)
    solution = jnp.concatenate(outputs[::-1], 0)
    return (solution, from_above)


def solution(mesh):
    placed = (
        P(("leaf", "front"), None),
        P(("leaf", "front"), None),
        P("leaf", "front"),
        P("front", "leaf"),
        P(),
    )
    return jax.shard_map(
        per_device,
        mesh=mesh,
        in_specs=placed,
        out_specs=(P(("leaf", "front"), None), P(("leaf", "front"), None)),
        check_vma=False,
    )
```

```python
import jax
import jax.numpy as jnp
from jax import lax
from jax.sharding import PartitionSpec as P

PIV = 4096
UPD = 1024
BLK = 128


def partner(block, axis, stride):
    count = lax.axis_size(axis)
    route = []
    for low in range(count):
        high = low | 1 << stride
        if high != low and high < count:
            route += [(low, high), (high, low)]
    return lax.ppermute(block, axis, route)


def child_base(leaves, height):
    total_rows = 0
    for depth in range(height - 1):
        total_rows = total_rows + leaves // 2**depth
    return total_rows


def list_row(extend_lists, row_index):
    return lax.dynamic_slice_in_dim(extend_lists, row_index, 1, 0)[0]


def upper_bit(position, bit_index):
    return position >> bit_index & 1 == 1


def joined(position, bit_index, portion, partner_rows):
    return jnp.where(
        upper_bit(position, bit_index),
        jnp.concatenate([partner_rows, portion], 0),
        jnp.concatenate([portion, partner_rows], 0),
    )


def gather_own(portion, height, position):
    for bit_index in range(height):
        partner_rows = partner(portion.astype(jnp.bfloat16), "leaf", bit_index).astype(
            portion.dtype
        )
        portion = joined(position, bit_index, portion, partner_rows)
    return portion


def sum_updates(summand, height):
    for bit_index in range(height):
        summand = summand + partner(summand.astype(jnp.bfloat16), "leaf", bit_index).astype(
            summand.dtype
        )
    return summand


def sum_solution(summand, height):
    for bit_index in range(height):
        summand = summand + partner(summand.astype(jnp.bfloat16), "leaf", bit_index).astype(
            summand.dtype
        )
    return summand


def front_sum(summand):
    bits = lax.axis_size("front").bit_length() - 1
    if summand.shape[0] < 1024:
        for bit_index in range(bits):
            half = summand.astype(jnp.bfloat16)
            summand = half.astype(jnp.float32) + partner(half, "front", bit_index).astype(
                jnp.float32
            )
        return summand
    column = lax.axis_index("front")
    for bit_index in range(bits):
        half_rows = summand.shape[0] // 2
        upper = column >> bit_index & 1
        keep = lax.dynamic_slice_in_dim(summand, upper * half_rows, half_rows, 0)
        send = lax.dynamic_slice_in_dim(summand, (1 - upper) * half_rows, half_rows, 0)
        summand = keep + partner(send.astype(jnp.bfloat16), "front", bit_index).astype(
            jnp.float32
        )
    summand = summand.astype(jnp.bfloat16)
    for bit_index in reversed(range(bits)):
        summand = joined(column, bit_index, summand, partner(summand, "front", bit_index))
    return summand.astype(jnp.float32)


def gather_all_own(upper_rhs, levels, position, piv_dev):
    pieces = {}
    for height in range(1, levels + 1):
        rhs_len = piv_dev // 2**height
        rhs_start = piv_dev - piv_dev // 2 ** (height - 1)
        pieces[height] = upper_rhs[rhs_start : rhs_start + rhs_len]
    for bit_index in range(levels):
        active = [height for height in range(bit_index + 1, levels + 1)]
        sent = jnp.concatenate([pieces[height] for height in active], 0)
        received = partner(sent.astype(jnp.bfloat16), "leaf", bit_index).astype(sent.dtype)
        offset = 0
        for height in active:
            count = pieces[height].shape[0]
            pieces[height] = joined(
                position, bit_index, pieces[height], received[offset : offset + count]
            )
            offset += count
    return pieces


def per_device(section_updates, upper_rhs, pivot_inverse, coupling, extend_lists):
    leaves = lax.axis_size("leaf")
    fronts = lax.axis_size("front")
    levels = leaves.bit_length() - 1
    position = lax.axis_index("leaf")
    column = lax.axis_index("front")
    rhs_width = upper_rhs.shape[1]
    piv_dev = PIV // fronts
    upd_dev = UPD // fronts
    piv_blocks = piv_dev // BLK
    upd_blocks = upd_dev // BLK
    block_count = UPD // BLK
    local_blocks = jnp.concatenate(
        [
            column * piv_blocks + jnp.arange(piv_blocks, dtype=jnp.int32),
            PIV // BLK + column * upd_blocks + jnp.arange(upd_blocks, dtype=jnp.int32),
        ]
    )
    local_count = piv_blocks + upd_blocks
    carried = section_updates
    own_pieces = gather_all_own(upper_rhs, levels, position, piv_dev)
    saved_part = []
    saved_half = []
    for height in range(1, levels + 1):
        group_size = 2**height
        span_rows = PIV // group_size
        band_start = PIV - PIV // 2 ** (height - 1)
        rhs_len = piv_dev // group_size
        rhs_start = piv_dev - piv_dev // 2 ** (height - 1)
        member = position & group_size - 1
        own_child = child_base(leaves, height) + (position >> height - 1)
        sibling = partner(carried, "leaf", height - 1)
        pair_blocks = lax.all_gather(jnp.stack([carried, sibling]), "front", axis=1, tiled=True)
        pair_lists = jnp.stack(
            [list_row(extend_lists, own_child), list_row(extend_lists, own_child ^ 1)]
        )
        chooser = (pair_lists.reshape(2 * block_count)[None, :] == local_blocks[:, None]).astype(
            jnp.bfloat16
        )
        assembled = jnp.dot(
            chooser,
            pair_blocks.reshape(2 * block_count, BLK * rhs_width),
            preferred_element_type=jnp.float32,
        ).reshape(local_count * BLK, rhs_width)
        own_rows = own_pieces[height]
        rows_half = (own_rows + assembled[:piv_dev]).astype(jnp.bfloat16)
        g_share = pivot_inverse[band_start : band_start + span_rows]
        pivot_part = front_sum(
            jnp.dot(g_share, rows_half, preferred_element_type=jnp.float32)
        )
        pivot_half = pivot_part.astype(jnp.bfloat16)
        saved_part.append(pivot_part)
        saved_half.append(pivot_half)
        if height < levels:
            c_share = coupling[:, band_start : band_start + span_rows]
            summand = jnp.dot(c_share, pivot_half, preferred_element_type=jnp.float32)
            frame_upd = assembled[piv_dev:]
            carried = (frame_upd - sum_updates(summand, height)).astype(jnp.bfloat16)
    from_above = carried
    outputs = []
    for height in range(levels, 0, -1):
        group_size = 2**height
        span_rows = PIV // group_size
        band_start = PIV - PIV // 2 ** (height - 1)
        member = position & group_size - 1
        pivot_part = saved_part[height - 1]
        if height < levels:
            c_share = coupling[:, band_start : band_start + span_rows]
            back_total = front_sum(
                jnp.einsum("up,ur->pr", c_share, from_above, preferred_element_type=jnp.float32)
            )
            weight_half = (pivot_part - back_total).astype(jnp.bfloat16)
            upper_rows = from_above
        else:
            weight_half = saved_half[height - 1]
            upper_rows = jnp.zeros((upd_dev, rhs_width), jnp.bfloat16)
        g_share = pivot_inverse[band_start : band_start + span_rows]
        solve_term = jnp.einsum(
            "cp,cr->pr", g_share, weight_half, preferred_element_type=jnp.float32
        )
        part_len = piv_dev // group_size
        summed = sum_solution(solve_term, height)
        portion = lax.dynamic_slice_in_dim(summed, member * part_len, part_len, 0)
        rows_half = summed.astype(jnp.bfloat16)
        outputs.append(portion)
        frame_half = jnp.concatenate([rows_half, upper_rows], 0).reshape(
            local_count, BLK * rhs_width
        )
        child_list = list_row(extend_lists, child_base(leaves, height) + (position >> height - 1))
        picker = (child_list[:, None] == local_blocks[None, :]).astype(jnp.bfloat16)
        outgoing = (
            jnp.dot(picker, frame_half, preferred_element_type=jnp.float32)
            .astype(jnp.bfloat16)
            .reshape(fronts, upd_dev, rhs_width)
        )
        incoming = lax.all_to_all(outgoing, "front", split_axis=0, concat_axis=0, tiled=True)
        from_above = jnp.sum(incoming, axis=0, dtype=jnp.float32).astype(jnp.bfloat16)
    solution = jnp.concatenate(outputs[::-1], 0)
    return (solution, from_above)


def solution(mesh):
    placed = (
        P(("leaf", "front"), None),
        P(("leaf", "front"), None),
        P("leaf", "front"),
        P("front", "leaf"),
        P(),
    )
    return jax.shard_map(
        per_device,
        mesh=mesh,
        in_specs=placed,
        out_specs=(P(("leaf", "front"), None), P(("leaf", "front"), None)),
        check_vma=False,
    )
```

```python
import jax
import jax.numpy as jnp
from jax import lax
from jax.sharding import PartitionSpec as P

PIV = 4096
UPD = 1024
BLK = 128


def partner(block, axis, stride):
    count = lax.axis_size(axis)
    route = []
    for low in range(count):
        high = low | 1 << stride
        if high != low and high < count:
            route += [(low, high), (high, low)]
    return lax.ppermute(block, axis, route)


def child_base(leaves, height):
    total_rows = 0
    for depth in range(height - 1):
        total_rows = total_rows + leaves // 2**depth
    return total_rows


def list_row(extend_lists, row_index):
    return lax.dynamic_slice_in_dim(extend_lists, row_index, 1, 0)[0]


def upper_bit(position, bit_index):
    return position >> bit_index & 1 == 1


def joined(position, bit_index, portion, partner_rows):
    return jnp.where(
        upper_bit(position, bit_index),
        jnp.concatenate([partner_rows, portion], 0),
        jnp.concatenate([portion, partner_rows], 0),
    )


def gather_own(portion, height, position):
    for bit_index in range(height):
        partner_rows = partner(portion.astype(jnp.bfloat16), "leaf", bit_index).astype(
            portion.dtype
        )
        portion = joined(position, bit_index, portion, partner_rows)
    return portion


def sum_updates(summand, height):
    for bit_index in range(height):
        summand = summand + partner(summand.astype(jnp.bfloat16), "leaf", bit_index).astype(
            summand.dtype
        )
    return summand


def sum_solution(summand, height):
    for bit_index in range(height):
        summand = summand + partner(summand.astype(jnp.bfloat16), "leaf", bit_index).astype(
            summand.dtype
        )
    return summand


def front_sum(summand):
    bits = lax.axis_size("front").bit_length() - 1
    if summand.shape[0] < 1024:
        for bit_index in range(bits):
            half = summand.astype(jnp.bfloat16)
            summand = half.astype(jnp.float32) + partner(half, "front", bit_index).astype(
                jnp.float32
            )
        return summand
    column = lax.axis_index("front")
    for bit_index in range(bits):
        half_rows = summand.shape[0] // 2
        upper = column >> bit_index & 1
        keep = lax.dynamic_slice_in_dim(summand, upper * half_rows, half_rows, 0)
        send = lax.dynamic_slice_in_dim(summand, (1 - upper) * half_rows, half_rows, 0)
        summand = keep + partner(send.astype(jnp.bfloat16), "front", bit_index).astype(
            jnp.float32
        )
    summand = summand.astype(jnp.bfloat16)
    for bit_index in reversed(range(bits)):
        summand = joined(column, bit_index, summand, partner(summand, "front", bit_index))
    return summand.astype(jnp.float32)


def front_gather(blocks):
    bits = lax.axis_size("front").bit_length() - 1
    column = lax.axis_index("front")
    for bit_index in reversed(range(bits)):
        received = partner(blocks, "front", bit_index)
        blocks = jnp.where(
            upper_bit(column, bit_index),
            jnp.concatenate([received, blocks], 1),
            jnp.concatenate([blocks, received], 1),
        )
    return blocks


def gathered_order(count):
    bits = count.bit_length() - 1
    return [int(format(index, f"0{bits}b")[::-1], 2) for index in range(count)]


def front_scatter_sum(outgoing):
    bits = lax.axis_size("front").bit_length() - 1
    column = lax.axis_index("front")
    rest = outgoing.shape[1:]
    split = outgoing.reshape((2,) * bits + rest)
    for bit_index in range(bits):
        axis = bits - 1 - bit_index
        mine = column >> bit_index & 1
        keep = lax.dynamic_index_in_dim(split, mine, axis, keepdims=False)
        send = lax.dynamic_index_in_dim(split, 1 - mine, axis, keepdims=False)
        received = partner(send, "front", bit_index)
        split = (keep.astype(jnp.float32) + received.astype(jnp.float32)).astype(outgoing.dtype)
    return split


def gather_all_own(upper_rhs, levels, position, piv_dev):
    pieces = {}
    for height in range(1, levels + 1):
        rhs_len = piv_dev // 2**height
        rhs_start = piv_dev - piv_dev // 2 ** (height - 1)
        pieces[height] = upper_rhs[rhs_start : rhs_start + rhs_len]
    for bit_index in range(levels):
        active = [height for height in range(bit_index + 1, levels + 1)]
        sent = jnp.concatenate([pieces[height] for height in active], 0)
        received = partner(sent.astype(jnp.bfloat16), "leaf", bit_index).astype(sent.dtype)
        offset = 0
        for height in active:
            count = pieces[height].shape[0]
            pieces[height] = joined(
                position, bit_index, pieces[height], received[offset : offset + count]
            )
            offset += count
    return pieces


def per_device(section_updates, upper_rhs, pivot_inverse, coupling, extend_lists):
    leaves = lax.axis_size("leaf")
    fronts = lax.axis_size("front")
    levels = leaves.bit_length() - 1
    position = lax.axis_index("leaf")
    column = lax.axis_index("front")
    rhs_width = upper_rhs.shape[1]
    piv_dev = PIV // fronts
    upd_dev = UPD // fronts
    piv_blocks = piv_dev // BLK
    upd_blocks = upd_dev // BLK
    block_count = UPD // BLK
    local_blocks = jnp.concatenate(
        [
            column * piv_blocks + jnp.arange(piv_blocks, dtype=jnp.int32),
            PIV // BLK + column * upd_blocks + jnp.arange(upd_blocks, dtype=jnp.int32),
        ]
    )
    local_count = piv_blocks + upd_blocks
    carried = section_updates
    own_pieces = gather_all_own(upper_rhs, levels, position, piv_dev)
    saved_part = []
    saved_half = []
    for height in range(1, levels + 1):
        group_size = 2**height
        span_rows = PIV // group_size
        band_start = PIV - PIV // 2 ** (height - 1)
        rhs_len = piv_dev // group_size
        rhs_start = piv_dev - piv_dev // 2 ** (height - 1)
        member = position & group_size - 1
        own_child = child_base(leaves, height) + (position >> height - 1)
        sibling = partner(carried, "leaf", height - 1)
        pair_blocks = front_gather(jnp.stack([carried, sibling]))
        pair_lists = jnp.stack(
            [list_row(extend_lists, own_child), list_row(extend_lists, own_child ^ 1)]
        )[:, jnp.array(gathered_order(fronts), jnp.int32)]
        chooser = (pair_lists.reshape(2 * block_count)[None, :] == local_blocks[:, None]).astype(
            jnp.bfloat16
        )
        assembled = jnp.dot(
            chooser,
            pair_blocks.reshape(2 * block_count, BLK * rhs_width),
            preferred_element_type=jnp.float32,
        ).reshape(local_count * BLK, rhs_width)
        own_rows = own_pieces[height]
        rows_half = (own_rows + assembled[:piv_dev]).astype(jnp.bfloat16)
        g_share = pivot_inverse[band_start : band_start + span_rows]
        pivot_part = front_sum(
            jnp.dot(g_share, rows_half, preferred_element_type=jnp.float32)
        )
        pivot_half = pivot_part.astype(jnp.bfloat16)
        saved_part.append(pivot_part)
        saved_half.append(pivot_half)
        if height < levels:
            c_share = coupling[:, band_start : band_start + span_rows]
            summand = jnp.dot(c_share, pivot_half, preferred_element_type=jnp.float32)
            frame_upd = assembled[piv_dev:]
            carried = (frame_upd - sum_updates(summand, height)).astype(jnp.bfloat16)
    from_above = carried
    outputs = []
    for height in range(levels, 0, -1):
        group_size = 2**height
        span_rows = PIV // group_size
        band_start = PIV - PIV // 2 ** (height - 1)
        member = position & group_size - 1
        pivot_part = saved_part[height - 1]
        if height < levels:
            c_share = coupling[:, band_start : band_start + span_rows]
            back_total = front_sum(
                jnp.einsum("up,ur->pr", c_share, from_above, preferred_element_type=jnp.float32)
            )
            weight_half = (pivot_part - back_total).astype(jnp.bfloat16)
            upper_rows = from_above
        else:
            weight_half = saved_half[height - 1]
            upper_rows = jnp.zeros((upd_dev, rhs_width), jnp.bfloat16)
        g_share = pivot_inverse[band_start : band_start + span_rows]
        solve_term = jnp.einsum(
            "cp,cr->pr", g_share, weight_half, preferred_element_type=jnp.float32
        )
        part_len = piv_dev // group_size
        summed = sum_solution(solve_term, height)
        portion = lax.dynamic_slice_in_dim(summed, member * part_len, part_len, 0)
        rows_half = summed.astype(jnp.bfloat16)
        outputs.append(portion)
        frame_half = jnp.concatenate([rows_half, upper_rows], 0).reshape(
            local_count, BLK * rhs_width
        )
        child_list = list_row(extend_lists, child_base(leaves, height) + (position >> height - 1))
        picker = (child_list[:, None] == local_blocks[None, :]).astype(jnp.bfloat16)
        outgoing = (
            jnp.dot(picker, frame_half, preferred_element_type=jnp.float32)
            .astype(jnp.bfloat16)
            .reshape(fronts, upd_dev, rhs_width)
        )
        from_above = front_scatter_sum(outgoing)
    solution = jnp.concatenate(outputs[::-1], 0)
    return (solution, from_above)


def solution(mesh):
    placed = (
        P(("leaf", "front"), None),
        P(("leaf", "front"), None),
        P("leaf", "front"),
        P("front", "leaf"),
        P(),
    )
    return jax.shard_map(
        per_device,
        mesh=mesh,
        in_specs=placed,
        out_specs=(P(("leaf", "front"), None), P(("leaf", "front"), None)),
        check_vma=False,
    )
```

```python
import jax
import jax.numpy as jnp
from jax import lax
from jax.sharding import PartitionSpec as P

PIV = 4096
UPD = 1024
BLK = 128


def partner(block, axis, stride):
    count = lax.axis_size(axis)
    route = []
    for low in range(count):
        high = low | 1 << stride
        if high != low and high < count:
            route += [(low, high), (high, low)]
    return lax.ppermute(block, axis, route)


def child_base(leaves, height):
    total_rows = 0
    for depth in range(height - 1):
        total_rows = total_rows + leaves // 2**depth
    return total_rows


def list_row(extend_lists, row_index):
    return lax.dynamic_slice_in_dim(extend_lists, row_index, 1, 0)[0]


def upper_bit(position, bit_index):
    return position >> bit_index & 1 == 1


def joined(position, bit_index, portion, partner_rows):
    return jnp.where(
        upper_bit(position, bit_index),
        jnp.concatenate([partner_rows, portion], 0),
        jnp.concatenate([portion, partner_rows], 0),
    )


def gather_own(portion, height, position):
    for bit_index in range(height):
        partner_rows = partner(portion.astype(jnp.bfloat16), "leaf", bit_index).astype(
            portion.dtype
        )
        portion = joined(position, bit_index, portion, partner_rows)
    return portion


def sum_updates(summand, height):
    for bit_index in range(height):
        summand = summand + partner(summand.astype(jnp.bfloat16), "leaf", bit_index).astype(
            summand.dtype
        )
    return summand


def sum_solution(summand, height):
    for bit_index in range(height):
        summand = summand + partner(summand.astype(jnp.bfloat16), "leaf", bit_index).astype(
            summand.dtype
        )
    return summand


def front_sum(summand):
    bits = lax.axis_size("front").bit_length() - 1
    if summand.shape[0] < 1024:
        for bit_index in range(bits):
            half = summand.astype(jnp.bfloat16)
            summand = half.astype(jnp.float32) + partner(half, "front", bit_index).astype(
                jnp.float32
            )
        return summand
    column = lax.axis_index("front")
    half_rows = summand.shape[0] // 2
    upper = column & 1
    keep = lax.dynamic_slice_in_dim(summand, upper * half_rows, half_rows, 0)
    send = lax.dynamic_slice_in_dim(summand, (1 - upper) * half_rows, half_rows, 0)
    summand = keep + partner(send.astype(jnp.bfloat16), "front", 0).astype(jnp.float32)
    for bit_index in range(1, bits):
        half = summand.astype(jnp.bfloat16)
        summand = half.astype(jnp.float32) + partner(half, "front", bit_index).astype(
            jnp.float32
        )
    summand = summand.astype(jnp.bfloat16)
    summand = joined(column, 0, summand, partner(summand, "front", 0))
    return summand.astype(jnp.float32)


def front_gather(blocks):
    bits = lax.axis_size("front").bit_length() - 1
    column = lax.axis_index("front")
    for bit_index in reversed(range(bits)):
        received = partner(blocks, "front", bit_index)
        blocks = jnp.where(
            upper_bit(column, bit_index),
            jnp.concatenate([received, blocks], 1),
            jnp.concatenate([blocks, received], 1),
        )
    return blocks


def gathered_order(count):
    bits = count.bit_length() - 1
    return [int(format(index, f"0{bits}b")[::-1], 2) for index in range(count)]


def front_scatter_sum(outgoing):
    bits = lax.axis_size("front").bit_length() - 1
    column = lax.axis_index("front")
    rest = outgoing.shape[1:]
    split = outgoing.reshape((2,) * bits + rest)
    for bit_index in range(bits):
        axis = bits - 1 - bit_index
        mine = column >> bit_index & 1
        keep = lax.dynamic_index_in_dim(split, mine, axis, keepdims=False)
        send = lax.dynamic_index_in_dim(split, 1 - mine, axis, keepdims=False)
        received = partner(send, "front", bit_index)
        split = (keep.astype(jnp.float32) + received.astype(jnp.float32)).astype(outgoing.dtype)
    return split


def gather_all_own(upper_rhs, levels, position, piv_dev):
    pieces = {}
    for height in range(1, levels + 1):
        rhs_len = piv_dev // 2**height
        rhs_start = piv_dev - piv_dev // 2 ** (height - 1)
        pieces[height] = upper_rhs[rhs_start : rhs_start + rhs_len]
    for bit_index in range(levels):
        active = [height for height in range(bit_index + 1, levels + 1)]
        sent = jnp.concatenate([pieces[height] for height in active], 0)
        received = partner(sent.astype(jnp.bfloat16), "leaf", bit_index).astype(sent.dtype)
        offset = 0
        for height in active:
            count = pieces[height].shape[0]
            pieces[height] = joined(
                position, bit_index, pieces[height], received[offset : offset + count]
            )
            offset += count
    return pieces


def per_device(section_updates, upper_rhs, pivot_inverse, coupling, extend_lists):
    leaves = lax.axis_size("leaf")
    fronts = lax.axis_size("front")
    levels = leaves.bit_length() - 1
    position = lax.axis_index("leaf")
    column = lax.axis_index("front")
    rhs_width = upper_rhs.shape[1]
    piv_dev = PIV // fronts
    upd_dev = UPD // fronts
    piv_blocks = piv_dev // BLK
    upd_blocks = upd_dev // BLK
    block_count = UPD // BLK
    local_blocks = jnp.concatenate(
        [
            column * piv_blocks + jnp.arange(piv_blocks, dtype=jnp.int32),
            PIV // BLK + column * upd_blocks + jnp.arange(upd_blocks, dtype=jnp.int32),
        ]
    )
    local_count = piv_blocks + upd_blocks
    carried = section_updates
    own_pieces = gather_all_own(upper_rhs, levels, position, piv_dev)
    saved_part = []
    saved_half = []
    for height in range(1, levels + 1):
        group_size = 2**height
        span_rows = PIV // group_size
        band_start = PIV - PIV // 2 ** (height - 1)
        rhs_len = piv_dev // group_size
        rhs_start = piv_dev - piv_dev // 2 ** (height - 1)
        member = position & group_size - 1
        own_child = child_base(leaves, height) + (position >> height - 1)
        sibling = partner(carried, "leaf", height - 1)
        pair_blocks = front_gather(jnp.stack([carried, sibling]))
        pair_lists = jnp.stack(
            [list_row(extend_lists, own_child), list_row(extend_lists, own_child ^ 1)]
        )[:, jnp.array(gathered_order(fronts), jnp.int32)]
        chooser = (pair_lists.reshape(2 * block_count)[None, :] == local_blocks[:, None]).astype(
            jnp.bfloat16
        )
        assembled = jnp.dot(
            chooser,
            pair_blocks.reshape(2 * block_count, BLK * rhs_width),
            preferred_element_type=jnp.float32,
        ).reshape(local_count * BLK, rhs_width)
        own_rows = own_pieces[height]
        rows_half = (own_rows + assembled[:piv_dev]).astype(jnp.bfloat16)
        g_share = pivot_inverse[band_start : band_start + span_rows]
        pivot_part = front_sum(
            jnp.dot(g_share, rows_half, preferred_element_type=jnp.float32)
        )
        pivot_half = pivot_part.astype(jnp.bfloat16)
        saved_part.append(pivot_part)
        saved_half.append(pivot_half)
        if height < levels:
            c_share = coupling[:, band_start : band_start + span_rows]
            summand = jnp.dot(c_share, pivot_half, preferred_element_type=jnp.float32)
            frame_upd = assembled[piv_dev:]
            carried = (frame_upd - sum_updates(summand, height)).astype(jnp.bfloat16)
    from_above = carried
    outputs = []
    for height in range(levels, 0, -1):
        group_size = 2**height
        span_rows = PIV // group_size
        band_start = PIV - PIV // 2 ** (height - 1)
        member = position & group_size - 1
        pivot_part = saved_part[height - 1]
        if height < levels:
            c_share = coupling[:, band_start : band_start + span_rows]
            back_total = front_sum(
                jnp.einsum("up,ur->pr", c_share, from_above, preferred_element_type=jnp.float32)
            )
            weight_half = (pivot_part - back_total).astype(jnp.bfloat16)
            upper_rows = from_above
        else:
            weight_half = saved_half[height - 1]
            upper_rows = jnp.zeros((upd_dev, rhs_width), jnp.bfloat16)
        g_share = pivot_inverse[band_start : band_start + span_rows]
        solve_term = jnp.einsum(
            "cp,cr->pr", g_share, weight_half, preferred_element_type=jnp.float32
        )
        part_len = piv_dev // group_size
        summed = sum_solution(solve_term, height)
        portion = lax.dynamic_slice_in_dim(summed, member * part_len, part_len, 0)
        rows_half = summed.astype(jnp.bfloat16)
        outputs.append(portion)
        frame_half = jnp.concatenate([rows_half, upper_rows], 0).reshape(
            local_count, BLK * rhs_width
        )
        child_list = list_row(extend_lists, child_base(leaves, height) + (position >> height - 1))
        picker = (child_list[:, None] == local_blocks[None, :]).astype(jnp.bfloat16)
        outgoing = (
            jnp.dot(picker, frame_half, preferred_element_type=jnp.float32)
            .astype(jnp.bfloat16)
            .reshape(fronts, upd_dev, rhs_width)
        )
        from_above = front_scatter_sum(outgoing)
    solution = jnp.concatenate(outputs[::-1], 0)
    return (solution, from_above)


def solution(mesh):
    placed = (
        P(("leaf", "front"), None),
        P(("leaf", "front"), None),
        P("leaf", "front"),
        P("front", "leaf"),
        P(),
    )
    return jax.shard_map(
        per_device,
        mesh=mesh,
        in_specs=placed,
        out_specs=(P(("leaf", "front"), None), P(("leaf", "front"), None)),
        check_vma=False,
    )
```

```python
import jax
import jax.numpy as jnp
from jax import lax
from jax.sharding import PartitionSpec as P

PIV = 4096
UPD = 1024
BLK = 128


def partner(block, axis, stride):
    count = lax.axis_size(axis)
    route = []
    for low in range(count):
        high = low | 1 << stride
        if high != low and high < count:
            route += [(low, high), (high, low)]
    return lax.ppermute(block, axis, route)


def child_base(leaves, height):
    total_rows = 0
    for depth in range(height - 1):
        total_rows = total_rows + leaves // 2**depth
    return total_rows


def list_row(extend_lists, row_index):
    return lax.dynamic_slice_in_dim(extend_lists, row_index, 1, 0)[0]


def upper_bit(position, bit_index):
    return position >> bit_index & 1 == 1


def joined(position, bit_index, portion, partner_rows):
    return jnp.where(
        upper_bit(position, bit_index),
        jnp.concatenate([partner_rows, portion], 0),
        jnp.concatenate([portion, partner_rows], 0),
    )


def gather_own(portion, height, position):
    for bit_index in range(height):
        partner_rows = partner(portion.astype(jnp.bfloat16), "leaf", bit_index).astype(
            portion.dtype
        )
        portion = joined(position, bit_index, portion, partner_rows)
    return portion


def sum_updates(summand, height):
    for bit_index in range(height):
        summand = summand + partner(summand.astype(jnp.bfloat16), "leaf", bit_index).astype(
            summand.dtype
        )
    return summand


def sum_solution(summand, height):
    for bit_index in range(height):
        summand = summand + partner(summand.astype(jnp.bfloat16), "leaf", bit_index).astype(
            summand.dtype
        )
    return summand


def front_sum(summand):
    bits = lax.axis_size("front").bit_length() - 1
    if summand.shape[0] < 1024:
        for bit_index in range(bits):
            half = summand.astype(jnp.bfloat16)
            summand = half.astype(jnp.float32) + partner(half, "front", bit_index).astype(
                jnp.float32
            )
        return summand
    column = lax.axis_index("front")
    half_rows = summand.shape[0] // 2
    upper = column & 1
    keep = lax.dynamic_slice_in_dim(summand, upper * half_rows, half_rows, 0)
    send = lax.dynamic_slice_in_dim(summand, (1 - upper) * half_rows, half_rows, 0)
    summand = keep + partner(send.astype(jnp.bfloat16), "front", 0).astype(jnp.float32)
    for bit_index in range(1, bits):
        half = summand.astype(jnp.bfloat16)
        summand = half.astype(jnp.float32) + partner(half, "front", bit_index).astype(
            jnp.float32
        )
    summand = summand.astype(jnp.bfloat16)
    summand = joined(column, 0, summand, partner(summand, "front", 0))
    return summand.astype(jnp.float32)


def front_gather(blocks):
    bits = lax.axis_size("front").bit_length() - 1
    column = lax.axis_index("front")
    for bit_index in reversed(range(bits)):
        received = partner(blocks, "front", bit_index)
        blocks = jnp.where(
            upper_bit(column, bit_index),
            jnp.concatenate([received, blocks], 1),
            jnp.concatenate([blocks, received], 1),
        )
    return blocks


def gathered_order(count):
    bits = count.bit_length() - 1
    return [int(format(index, f"0{bits}b")[::-1], 2) for index in range(count)]


def front_scatter_sum(outgoing):
    bits = lax.axis_size("front").bit_length() - 1
    column = lax.axis_index("front")
    rest = outgoing.shape[1:]
    split = outgoing.reshape((2,) * bits + rest)
    for bit_index in range(bits):
        axis = bits - 1 - bit_index
        mine = column >> bit_index & 1
        keep = lax.dynamic_index_in_dim(split, mine, axis, keepdims=False)
        send = lax.dynamic_index_in_dim(split, 1 - mine, axis, keepdims=False)
        received = partner(send, "front", bit_index)
        split = (keep.astype(jnp.float32) + received.astype(jnp.float32)).astype(outgoing.dtype)
    return split


def own_pieces_of(upper_rhs, levels, piv_dev):
    pieces = {}
    for height in range(1, levels + 1):
        rhs_len = piv_dev // 2**height
        rhs_start = piv_dev - piv_dev // 2 ** (height - 1)
        pieces[height] = upper_rhs[rhs_start : rhs_start + rhs_len]
    return pieces


def exchange_round(pieces, levels, position, bit_index, carried=None):
    active = [height for height in range(bit_index + 1, levels + 1)]
    parts = [pieces[height].astype(jnp.bfloat16) for height in active]
    if carried is not None:
        parts = [carried] + parts
    received = partner(jnp.concatenate(parts, 0), "leaf", bit_index)
    offset = 0
    sibling = None
    if carried is not None:
        sibling = received[: carried.shape[0]]
        offset = carried.shape[0]
    for height in active:
        count = pieces[height].shape[0]
        pieces[height] = joined(
            position,
            bit_index,
            pieces[height],
            received[offset : offset + count].astype(pieces[height].dtype),
        )
        offset += count
    return sibling


def per_device(section_updates, upper_rhs, pivot_inverse, coupling, extend_lists):
    leaves = lax.axis_size("leaf")
    fronts = lax.axis_size("front")
    levels = leaves.bit_length() - 1
    position = lax.axis_index("leaf")
    column = lax.axis_index("front")
    rhs_width = upper_rhs.shape[1]
    piv_dev = PIV // fronts
    upd_dev = UPD // fronts
    piv_blocks = piv_dev // BLK
    upd_blocks = upd_dev // BLK
    block_count = UPD // BLK
    local_blocks = jnp.concatenate(
        [
            column * piv_blocks + jnp.arange(piv_blocks, dtype=jnp.int32),
            PIV // BLK + column * upd_blocks + jnp.arange(upd_blocks, dtype=jnp.int32),
        ]
    )
    local_count = piv_blocks + upd_blocks
    carried = section_updates
    own_pieces = own_pieces_of(upper_rhs, levels, piv_dev)
    exchange_round(own_pieces, levels, position, 0)
    saved_part = []
    saved_half = []
    for height in range(1, levels + 1):
        group_size = 2**height
        span_rows = PIV // group_size
        band_start = PIV - PIV // 2 ** (height - 1)
        rhs_len = piv_dev // group_size
        rhs_start = piv_dev - piv_dev // 2 ** (height - 1)
        member = position & group_size - 1
        own_child = child_base(leaves, height) + (position >> height - 1)
        if height == 1:
            sibling = partner(carried, "leaf", height - 1)
        else:
            sibling = exchange_round(own_pieces, levels, position, height - 1, carried)
        pair_blocks = front_gather(jnp.stack([carried, sibling]))
        pair_lists = jnp.stack(
            [list_row(extend_lists, own_child), list_row(extend_lists, own_child ^ 1)]
        )[:, jnp.array(gathered_order(fronts), jnp.int32)]
        chooser = (pair_lists.reshape(2 * block_count)[None, :] == local_blocks[:, None]).astype(
            jnp.bfloat16
        )
        assembled = jnp.dot(
            chooser,
            pair_blocks.reshape(2 * block_count, BLK * rhs_width),
            preferred_element_type=jnp.float32,
        ).reshape(local_count * BLK, rhs_width)
        own_rows = own_pieces[height]
        rows_half = (own_rows + assembled[:piv_dev]).astype(jnp.bfloat16)
        g_share = pivot_inverse[band_start : band_start + span_rows]
        pivot_part = front_sum(
            jnp.dot(g_share, rows_half, preferred_element_type=jnp.float32)
        )
        pivot_half = pivot_part.astype(jnp.bfloat16)
        saved_part.append(pivot_part)
        saved_half.append(pivot_half)
        if height < levels:
            c_share = coupling[:, band_start : band_start + span_rows]
            summand = jnp.dot(c_share, pivot_half, preferred_element_type=jnp.float32)
            frame_upd = assembled[piv_dev:]
            carried = (frame_upd - sum_updates(summand, height)).astype(jnp.bfloat16)
    from_above = carried
    outputs = []
    for height in range(levels, 0, -1):
        group_size = 2**height
        span_rows = PIV // group_size
        band_start = PIV - PIV // 2 ** (height - 1)
        member = position & group_size - 1
        pivot_part = saved_part[height - 1]
        if height < levels:
            c_share = coupling[:, band_start : band_start + span_rows]
            back_total = front_sum(
                jnp.einsum("up,ur->pr", c_share, from_above, preferred_element_type=jnp.float32)
            )
            weight_half = (pivot_part - back_total).astype(jnp.bfloat16)
            upper_rows = from_above
        else:
            weight_half = saved_half[height - 1]
            upper_rows = jnp.zeros((upd_dev, rhs_width), jnp.bfloat16)
        g_share = pivot_inverse[band_start : band_start + span_rows]
        solve_term = jnp.einsum(
            "cp,cr->pr", g_share, weight_half, preferred_element_type=jnp.float32
        )
        part_len = piv_dev // group_size
        summed = sum_solution(solve_term, height)
        portion = lax.dynamic_slice_in_dim(summed, member * part_len, part_len, 0)
        rows_half = summed.astype(jnp.bfloat16)
        outputs.append(portion)
        frame_half = jnp.concatenate([rows_half, upper_rows], 0).reshape(
            local_count, BLK * rhs_width
        )
        child_list = list_row(extend_lists, child_base(leaves, height) + (position >> height - 1))
        picker = (child_list[:, None] == local_blocks[None, :]).astype(jnp.bfloat16)
        outgoing = (
            jnp.dot(picker, frame_half, preferred_element_type=jnp.float32)
            .astype(jnp.bfloat16)
            .reshape(fronts, upd_dev, rhs_width)
        )
        from_above = front_scatter_sum(outgoing)
    solution = jnp.concatenate(outputs[::-1], 0)
    return (solution, from_above)


def solution(mesh):
    placed = (
        P(("leaf", "front"), None),
        P(("leaf", "front"), None),
        P("leaf", "front"),
        P("front", "leaf"),
        P(),
    )
    return jax.shard_map(
        per_device,
        mesh=mesh,
        in_specs=placed,
        out_specs=(P(("leaf", "front"), None), P(("leaf", "front"), None)),
        check_vma=False,
    )
```

```python
import jax
import jax.numpy as jnp
from jax import lax
from jax.sharding import PartitionSpec as P

PIV = 4096
UPD = 1024
BLK = 128


def partner(block, axis, stride):
    count = lax.axis_size(axis)
    route = []
    for low in range(count):
        high = low | 1 << stride
        if high != low and high < count:
            route += [(low, high), (high, low)]
    return lax.ppermute(block, axis, route)


def child_base(leaves, height):
    total_rows = 0
    for depth in range(height - 1):
        total_rows = total_rows + leaves // 2**depth
    return total_rows


def list_row(extend_lists, row_index):
    return lax.dynamic_slice_in_dim(extend_lists, row_index, 1, 0)[0]


def upper_bit(position, bit_index):
    return position >> bit_index & 1 == 1


def joined(position, bit_index, portion, partner_rows):
    return jnp.where(
        upper_bit(position, bit_index),
        jnp.concatenate([partner_rows, portion], 0),
        jnp.concatenate([portion, partner_rows], 0),
    )


def gather_own(portion, height, position):
    for bit_index in range(height):
        partner_rows = partner(portion.astype(jnp.bfloat16), "leaf", bit_index).astype(
            portion.dtype
        )
        portion = joined(position, bit_index, portion, partner_rows)
    return portion


def sum_updates(summand, height):
    for bit_index in range(height):
        summand = summand + partner(summand.astype(jnp.bfloat16), "leaf", bit_index).astype(
            summand.dtype
        )
    return summand


def sum_solution(summand, height):
    for bit_index in range(height):
        summand = summand + partner(summand.astype(jnp.bfloat16), "leaf", bit_index).astype(
            summand.dtype
        )
    return summand


def front_sum(summand):
    bits = lax.axis_size("front").bit_length() - 1
    if summand.shape[0] < 1024:
        for bit_index in range(bits):
            half = summand.astype(jnp.bfloat16)
            summand = half.astype(jnp.float32) + partner(half, "front", bit_index).astype(
                jnp.float32
            )
        return summand
    column = lax.axis_index("front")
    half_rows = summand.shape[0] // 2
    upper = column & 1
    keep = lax.dynamic_slice_in_dim(summand, upper * half_rows, half_rows, 0)
    send = lax.dynamic_slice_in_dim(summand, (1 - upper) * half_rows, half_rows, 0)
    summand = keep + partner(send.astype(jnp.bfloat16), "front", 0).astype(jnp.float32)
    for bit_index in range(1, bits):
        half = summand.astype(jnp.bfloat16)
        summand = half.astype(jnp.float32) + partner(half, "front", bit_index).astype(
            jnp.float32
        )
    summand = summand.astype(jnp.bfloat16)
    summand = joined(column, 0, summand, partner(summand, "front", 0))
    return summand.astype(jnp.float32)


def front_gather(blocks):
    bits = lax.axis_size("front").bit_length() - 1
    column = lax.axis_index("front")
    for bit_index in reversed(range(bits)):
        received = partner(blocks, "front", bit_index)
        blocks = jnp.where(
            upper_bit(column, bit_index),
            jnp.concatenate([received, blocks], 1),
            jnp.concatenate([blocks, received], 1),
        )
    return blocks


def gathered_order(count):
    bits = count.bit_length() - 1
    return [int(format(index, f"0{bits}b")[::-1], 2) for index in range(count)]


def front_scatter_sum(outgoing):
    bits = lax.axis_size("front").bit_length() - 1
    column = lax.axis_index("front")
    rest = outgoing.shape[1:]
    split = outgoing.reshape((2,) * bits + rest)
    for bit_index in range(bits):
        axis = bits - 1 - bit_index
        mine = column >> bit_index & 1
        keep = lax.dynamic_index_in_dim(split, mine, axis, keepdims=False)
        send = lax.dynamic_index_in_dim(split, 1 - mine, axis, keepdims=False)
        received = partner(send, "front", bit_index)
        split = (keep.astype(jnp.float32) + received.astype(jnp.float32)).astype(outgoing.dtype)
    return split


def own_pieces_of(upper_rhs, levels, piv_dev):
    pieces = {}
    for height in range(1, levels + 1):
        rhs_len = piv_dev // 2**height
        rhs_start = piv_dev - piv_dev // 2 ** (height - 1)
        pieces[height] = upper_rhs[rhs_start : rhs_start + rhs_len]
    return pieces


def exchange_round(pieces, levels, position, bit_index, carried=None):
    active = [height for height in range(bit_index + 1, levels + 1)]
    parts = [pieces[height].astype(jnp.bfloat16) for height in active]
    if carried is not None:
        parts = [carried] + parts
    received = partner(jnp.concatenate(parts, 0), "leaf", bit_index)
    offset = 0
    sibling = None
    if carried is not None:
        sibling = received[: carried.shape[0]]
        offset = carried.shape[0]
    for height in active:
        count = pieces[height].shape[0]
        pieces[height] = joined(
            position,
            bit_index,
            pieces[height],
            received[offset : offset + count].astype(pieces[height].dtype),
        )
        offset += count
    return sibling


def per_device(section_updates, upper_rhs, pivot_inverse, coupling, extend_lists):
    leaves = lax.axis_size("leaf")
    fronts = lax.axis_size("front")
    levels = leaves.bit_length() - 1
    position = lax.axis_index("leaf")
    column = lax.axis_index("front")
    rhs_width = upper_rhs.shape[1]
    piv_dev = PIV // fronts
    upd_dev = UPD // fronts
    piv_blocks = piv_dev // BLK
    upd_blocks = upd_dev // BLK
    block_count = UPD // BLK
    local_blocks = jnp.concatenate(
        [
            column * piv_blocks + jnp.arange(piv_blocks, dtype=jnp.int32),
            PIV // BLK + column * upd_blocks + jnp.arange(upd_blocks, dtype=jnp.int32),
        ]
    )
    local_count = piv_blocks + upd_blocks
    carried = section_updates
    own_pieces = own_pieces_of(upper_rhs, levels, piv_dev)
    exchange_round(own_pieces, levels, position, 0)
    saved_part = []
    saved_half = []
    for height in range(1, levels + 1):
        group_size = 2**height
        span_rows = PIV // group_size
        band_start = PIV - PIV // 2 ** (height - 1)
        rhs_len = piv_dev // group_size
        rhs_start = piv_dev - piv_dev // 2 ** (height - 1)
        member = position & group_size - 1
        own_child = child_base(leaves, height) + (position >> height - 1)
        if height == 1:
            sibling = partner(carried, "leaf", height - 1)
        else:
            sibling = exchange_round(own_pieces, levels, position, height - 1, carried)
        pair_blocks = jnp.concatenate(
            [front_gather(carried[None]), front_gather(sibling[None])], 0
        )
        pair_lists = jnp.stack(
            [list_row(extend_lists, own_child), list_row(extend_lists, own_child ^ 1)]
        )[:, jnp.array(gathered_order(fronts), jnp.int32)]
        chooser = (pair_lists.reshape(2 * block_count)[None, :] == local_blocks[:, None]).astype(
            jnp.bfloat16
        )
        assembled = jnp.dot(
            chooser,
            pair_blocks.reshape(2 * block_count, BLK * rhs_width),
            preferred_element_type=jnp.float32,
        ).reshape(local_count * BLK, rhs_width)
        own_rows = own_pieces[height]
        rows_half = (own_rows + assembled[:piv_dev]).astype(jnp.bfloat16)
        g_share = pivot_inverse[band_start : band_start + span_rows]
        pivot_part = front_sum(
            jnp.dot(g_share, rows_half, preferred_element_type=jnp.float32)
        )
        pivot_half = pivot_part.astype(jnp.bfloat16)
        saved_part.append(pivot_part)
        saved_half.append(pivot_half)
        if height < levels:
            c_share = coupling[:, band_start : band_start + span_rows]
            summand = jnp.dot(c_share, pivot_half, preferred_element_type=jnp.float32)
            frame_upd = assembled[piv_dev:]
            carried = (frame_upd - sum_updates(summand, height)).astype(jnp.bfloat16)
    from_above = carried
    outputs = []
    for height in range(levels, 0, -1):
        group_size = 2**height
        span_rows = PIV // group_size
        band_start = PIV - PIV // 2 ** (height - 1)
        member = position & group_size - 1
        pivot_part = saved_part[height - 1]
        if height < levels:
            c_share = coupling[:, band_start : band_start + span_rows]
            back_total = front_sum(
                jnp.einsum("up,ur->pr", c_share, from_above, preferred_element_type=jnp.float32)
            )
            weight_half = (pivot_part - back_total).astype(jnp.bfloat16)
            upper_rows = from_above
        else:
            weight_half = saved_half[height - 1]
            upper_rows = jnp.zeros((upd_dev, rhs_width), jnp.bfloat16)
        g_share = pivot_inverse[band_start : band_start + span_rows]
        solve_term = jnp.einsum(
            "cp,cr->pr", g_share, weight_half, preferred_element_type=jnp.float32
        )
        part_len = piv_dev // group_size
        summed = sum_solution(solve_term, height)
        portion = lax.dynamic_slice_in_dim(summed, member * part_len, part_len, 0)
        rows_half = summed.astype(jnp.bfloat16)
        outputs.append(portion)
        frame_half = jnp.concatenate([rows_half, upper_rows], 0).reshape(
            local_count, BLK * rhs_width
        )
        child_list = list_row(extend_lists, child_base(leaves, height) + (position >> height - 1))
        picker = (child_list[:, None] == local_blocks[None, :]).astype(jnp.bfloat16)
        outgoing = (
            jnp.dot(picker, frame_half, preferred_element_type=jnp.float32)
            .astype(jnp.bfloat16)
            .reshape(fronts, upd_dev, rhs_width)
        )
        from_above = front_scatter_sum(outgoing)
    solution = jnp.concatenate(outputs[::-1], 0)
    return (solution, from_above)


def solution(mesh):
    placed = (
        P(("leaf", "front"), None),
        P(("leaf", "front"), None),
        P("leaf", "front"),
        P("front", "leaf"),
        P(),
    )
    return jax.shard_map(
        per_device,
        mesh=mesh,
        in_specs=placed,
        out_specs=(P(("leaf", "front"), None), P(("leaf", "front"), None)),
        check_vma=False,
    )
```

```python
import jax
import jax.numpy as jnp
from jax import lax
from jax.sharding import PartitionSpec as P

PIV = 4096
UPD = 1024
BLK = 128


def partner(block, axis, stride):
    count = lax.axis_size(axis)
    route = []
    for low in range(count):
        high = low | 1 << stride
        if high != low and high < count:
            route += [(low, high), (high, low)]
    return lax.ppermute(block, axis, route)


def child_base(leaves, height):
    total_rows = 0
    for depth in range(height - 1):
        total_rows = total_rows + leaves // 2**depth
    return total_rows


def list_row(extend_lists, row_index):
    return lax.dynamic_slice_in_dim(extend_lists, row_index, 1, 0)[0]


def upper_bit(position, bit_index):
    return position >> bit_index & 1 == 1


def joined(position, bit_index, portion, partner_rows):
    return jnp.where(
        upper_bit(position, bit_index),
        jnp.concatenate([partner_rows, portion], 0),
        jnp.concatenate([portion, partner_rows], 0),
    )


def gather_own(portion, height, position):
    for bit_index in range(height):
        partner_rows = partner(portion.astype(jnp.bfloat16), "leaf", bit_index).astype(
            portion.dtype
        )
        portion = joined(position, bit_index, portion, partner_rows)
    return portion


def sum_updates(summand, height):
    for bit_index in range(height):
        summand = summand + partner(summand.astype(jnp.bfloat16), "leaf", bit_index).astype(
            summand.dtype
        )
    return summand


def sum_solution(summand, height):
    for bit_index in range(height):
        summand = summand + partner(summand.astype(jnp.bfloat16), "leaf", bit_index).astype(
            summand.dtype
        )
    return summand


def front_sum(summand):
    bits = lax.axis_size("front").bit_length() - 1
    if summand.shape[0] < 512:
        for bit_index in range(bits):
            half = summand.astype(jnp.bfloat16)
            summand = half.astype(jnp.float32) + partner(half, "front", bit_index).astype(
                jnp.float32
            )
        return summand
    column = lax.axis_index("front")
    half_rows = summand.shape[0] // 2
    upper = column & 1
    keep = lax.dynamic_slice_in_dim(summand, upper * half_rows, half_rows, 0)
    send = lax.dynamic_slice_in_dim(summand, (1 - upper) * half_rows, half_rows, 0)
    summand = keep + partner(send.astype(jnp.bfloat16), "front", 0).astype(jnp.float32)
    for bit_index in range(1, bits):
        half = summand.astype(jnp.bfloat16)
        summand = half.astype(jnp.float32) + partner(half, "front", bit_index).astype(
            jnp.float32
        )
    summand = summand.astype(jnp.bfloat16)
    summand = joined(column, 0, summand, partner(summand, "front", 0))
    return summand.astype(jnp.float32)


def front_gather(blocks):
    bits = lax.axis_size("front").bit_length() - 1
    column = lax.axis_index("front")
    for bit_index in reversed(range(bits)):
        received = partner(blocks, "front", bit_index)
        blocks = jnp.where(
            upper_bit(column, bit_index),
            jnp.concatenate([received, blocks], 1),
            jnp.concatenate([blocks, received], 1),
        )
    return blocks


def gathered_order(count):
    bits = count.bit_length() - 1
    return [int(format(index, f"0{bits}b")[::-1], 2) for index in range(count)]


def front_scatter_sum(outgoing):
    bits = lax.axis_size("front").bit_length() - 1
    column = lax.axis_index("front")
    rest = outgoing.shape[1:]
    split = outgoing.reshape((2,) * bits + rest)
    for bit_index in range(bits):
        axis = bits - 1 - bit_index
        mine = column >> bit_index & 1
        keep = lax.dynamic_index_in_dim(split, mine, axis, keepdims=False)
        send = lax.dynamic_index_in_dim(split, 1 - mine, axis, keepdims=False)
        received = partner(send, "front", bit_index)
        split = (keep.astype(jnp.float32) + received.astype(jnp.float32)).astype(outgoing.dtype)
    return split


def own_pieces_of(upper_rhs, levels, piv_dev):
    pieces = {}
    for height in range(1, levels + 1):
        rhs_len = piv_dev // 2**height
        rhs_start = piv_dev - piv_dev // 2 ** (height - 1)
        pieces[height] = upper_rhs[rhs_start : rhs_start + rhs_len]
    return pieces


def exchange_round(pieces, levels, position, bit_index, carried=None):
    active = [height for height in range(bit_index + 1, levels + 1)]
    parts = [pieces[height].astype(jnp.bfloat16) for height in active]
    if carried is not None:
        parts = [carried] + parts
    received = partner(jnp.concatenate(parts, 0), "leaf", bit_index)
    offset = 0
    sibling = None
    if carried is not None:
        sibling = received[: carried.shape[0]]
        offset = carried.shape[0]
    for height in active:
        count = pieces[height].shape[0]
        pieces[height] = joined(
            position,
            bit_index,
            pieces[height],
            received[offset : offset + count].astype(pieces[height].dtype),
        )
        offset += count
    return sibling


def per_device(section_updates, upper_rhs, pivot_inverse, coupling, extend_lists):
    leaves = lax.axis_size("leaf")
    fronts = lax.axis_size("front")
    levels = leaves.bit_length() - 1
    position = lax.axis_index("leaf")
    column = lax.axis_index("front")
    rhs_width = upper_rhs.shape[1]
    piv_dev = PIV // fronts
    upd_dev = UPD // fronts
    piv_blocks = piv_dev // BLK
    upd_blocks = upd_dev // BLK
    block_count = UPD // BLK
    local_blocks = jnp.concatenate(
        [
            column * piv_blocks + jnp.arange(piv_blocks, dtype=jnp.int32),
            PIV // BLK + column * upd_blocks + jnp.arange(upd_blocks, dtype=jnp.int32),
        ]
    )
    local_count = piv_blocks + upd_blocks
    carried = section_updates
    own_pieces = own_pieces_of(upper_rhs, levels, piv_dev)
    exchange_round(own_pieces, levels, position, 0)
    saved_part = []
    saved_half = []
    for height in range(1, levels + 1):
        group_size = 2**height
        span_rows = PIV // group_size
        band_start = PIV - PIV // 2 ** (height - 1)
        rhs_len = piv_dev // group_size
        rhs_start = piv_dev - piv_dev // 2 ** (height - 1)
        member = position & group_size - 1
        own_child = child_base(leaves, height) + (position >> height - 1)
        if height == 1:
            sibling = partner(carried, "leaf", height - 1)
        else:
            sibling = exchange_round(own_pieces, levels, position, height - 1, carried)
        pair_blocks = jnp.concatenate(
            [front_gather(carried[None]), front_gather(sibling[None])], 0
        )
        pair_lists = jnp.stack(
            [list_row(extend_lists, own_child), list_row(extend_lists, own_child ^ 1)]
        )[:, jnp.array(gathered_order(fronts), jnp.int32)]
        chooser = (pair_lists.reshape(2 * block_count)[None, :] == local_blocks[:, None]).astype(
            jnp.bfloat16
        )
        assembled = jnp.dot(
            chooser,
            pair_blocks.reshape(2 * block_count, BLK * rhs_width),
            preferred_element_type=jnp.float32,
        ).reshape(local_count * BLK, rhs_width)
        own_rows = own_pieces[height]
        rows_half = (own_rows + assembled[:piv_dev]).astype(jnp.bfloat16)
        g_share = pivot_inverse[band_start : band_start + span_rows]
        pivot_part = front_sum(
            jnp.dot(g_share, rows_half, preferred_element_type=jnp.float32)
        )
        pivot_half = pivot_part.astype(jnp.bfloat16)
        saved_part.append(pivot_part)
        saved_half.append(pivot_half)
        if height < levels:
            c_share = coupling[:, band_start : band_start + span_rows]
            summand = jnp.dot(c_share, pivot_half, preferred_element_type=jnp.float32)
            frame_upd = assembled[piv_dev:]
            carried = (frame_upd - sum_updates(summand, height)).astype(jnp.bfloat16)
    from_above = carried
    outputs = []
    for height in range(levels, 0, -1):
        group_size = 2**height
        span_rows = PIV // group_size
        band_start = PIV - PIV // 2 ** (height - 1)
        member = position & group_size - 1
        pivot_part = saved_part[height - 1]
        if height < levels:
            c_share = coupling[:, band_start : band_start + span_rows]
            back_total = front_sum(
                jnp.einsum("up,ur->pr", c_share, from_above, preferred_element_type=jnp.float32)
            )
            weight_half = (pivot_part - back_total).astype(jnp.bfloat16)
            upper_rows = from_above
        else:
            weight_half = saved_half[height - 1]
            upper_rows = jnp.zeros((upd_dev, rhs_width), jnp.bfloat16)
        g_share = pivot_inverse[band_start : band_start + span_rows]
        solve_term = jnp.einsum(
            "cp,cr->pr", g_share, weight_half, preferred_element_type=jnp.float32
        )
        part_len = piv_dev // group_size
        summed = sum_solution(solve_term, height)
        portion = lax.dynamic_slice_in_dim(summed, member * part_len, part_len, 0)
        rows_half = summed.astype(jnp.bfloat16)
        outputs.append(portion)
        frame_half = jnp.concatenate([rows_half, upper_rows], 0).reshape(
            local_count, BLK * rhs_width
        )
        child_list = list_row(extend_lists, child_base(leaves, height) + (position >> height - 1))
        picker = (child_list[:, None] == local_blocks[None, :]).astype(jnp.bfloat16)
        outgoing = (
            jnp.dot(picker, frame_half, preferred_element_type=jnp.float32)
            .astype(jnp.bfloat16)
            .reshape(fronts, upd_dev, rhs_width)
        )
        from_above = front_scatter_sum(outgoing)
    solution = jnp.concatenate(outputs[::-1], 0)
    return (solution, from_above)


def solution(mesh):
    placed = (
        P(("leaf", "front"), None),
        P(("leaf", "front"), None),
        P("leaf", "front"),
        P("front", "leaf"),
        P(),
    )
    return jax.shard_map(
        per_device,
        mesh=mesh,
        in_specs=placed,
        out_specs=(P(("leaf", "front"), None), P(("leaf", "front"), None)),
        check_vma=False,
    )
```

```python
import jax
import jax.numpy as jnp
from jax import lax
from jax.sharding import PartitionSpec as P

PIV = 4096
UPD = 1024
BLK = 128


def partner(block, axis, stride):
    count = lax.axis_size(axis)
    route = []
    for low in range(count):
        high = low | 1 << stride
        if high != low and high < count:
            route += [(low, high), (high, low)]
    return lax.ppermute(block, axis, route)


def child_base(leaves, height):
    total_rows = 0
    for depth in range(height - 1):
        total_rows = total_rows + leaves // 2**depth
    return total_rows


def list_row(extend_lists, row_index):
    return lax.dynamic_slice_in_dim(extend_lists, row_index, 1, 0)[0]


def upper_bit(position, bit_index):
    return position >> bit_index & 1 == 1


def joined(position, bit_index, portion, partner_rows):
    return jnp.where(
        upper_bit(position, bit_index),
        jnp.concatenate([partner_rows, portion], 0),
        jnp.concatenate([portion, partner_rows], 0),
    )


def gather_own(portion, height, position):
    for bit_index in range(height):
        partner_rows = partner(portion.astype(jnp.bfloat16), "leaf", bit_index).astype(
            portion.dtype
        )
        portion = joined(position, bit_index, portion, partner_rows)
    return portion


def sum_updates(summand, height):
    for bit_index in range(height):
        summand = summand + partner(summand.astype(jnp.bfloat16), "leaf", bit_index).astype(
            summand.dtype
        )
    return summand


def sum_solution(summand, height):
    for bit_index in range(height):
        summand = summand + partner(summand.astype(jnp.bfloat16), "leaf", bit_index).astype(
            summand.dtype
        )
    return summand


def front_sum(summand):
    bits = lax.axis_size("front").bit_length() - 1
    if summand.shape[0] < 512:
        for bit_index in range(bits):
            half = summand.astype(jnp.bfloat16)
            summand = half.astype(jnp.float32) + partner(half, "front", bit_index).astype(
                jnp.float32
            )
        return summand
    column = lax.axis_index("front")
    half_rows = summand.shape[0] // 2
    upper = column & 1
    keep = lax.dynamic_slice_in_dim(summand, upper * half_rows, half_rows, 0)
    send = lax.dynamic_slice_in_dim(summand, (1 - upper) * half_rows, half_rows, 0)
    summand = keep + partner(send.astype(jnp.bfloat16), "front", 0).astype(jnp.float32)
    for bit_index in range(1, bits):
        half = summand.astype(jnp.bfloat16)
        summand = half.astype(jnp.float32) + partner(half, "front", bit_index).astype(
            jnp.float32
        )
    summand = summand.astype(jnp.bfloat16)
    summand = joined(column, 0, summand, partner(summand, "front", 0))
    return summand.astype(jnp.float32)


def front_gather(blocks):
    bits = lax.axis_size("front").bit_length() - 1
    for bit_index in reversed(range(bits)):
        blocks = jnp.concatenate([blocks, partner(blocks, "front", bit_index)], 1)
    return blocks


def gathered_order(count):
    bits = count.bit_length() - 1
    return [int(format(index, f"0{bits}b")[::-1], 2) for index in range(count)]


def front_scatter_sum(outgoing):
    bits = lax.axis_size("front").bit_length() - 1
    column = lax.axis_index("front")
    rest = outgoing.shape[1:]
    split = outgoing.reshape((2,) * bits + rest)
    for bit_index in range(bits):
        axis = bits - 1 - bit_index
        mine = column >> bit_index & 1
        keep = lax.dynamic_index_in_dim(split, mine, axis, keepdims=False)
        send = lax.dynamic_index_in_dim(split, 1 - mine, axis, keepdims=False)
        received = partner(send, "front", bit_index)
        split = (keep.astype(jnp.float32) + received.astype(jnp.float32)).astype(outgoing.dtype)
    return split


def own_pieces_of(upper_rhs, levels, piv_dev):
    pieces = {}
    for height in range(1, levels + 1):
        rhs_len = piv_dev // 2**height
        rhs_start = piv_dev - piv_dev // 2 ** (height - 1)
        pieces[height] = upper_rhs[rhs_start : rhs_start + rhs_len]
    return pieces


def exchange_round(pieces, levels, position, bit_index, carried=None):
    active = [height for height in range(bit_index + 1, levels + 1)]
    parts = [pieces[height].astype(jnp.bfloat16) for height in active]
    if carried is not None:
        parts = [carried] + parts
    received = partner(jnp.concatenate(parts, 0), "leaf", bit_index)
    offset = 0
    sibling = None
    if carried is not None:
        sibling = received[: carried.shape[0]]
        offset = carried.shape[0]
    for height in active:
        count = pieces[height].shape[0]
        pieces[height] = joined(
            position,
            bit_index,
            pieces[height],
            received[offset : offset + count].astype(pieces[height].dtype),
        )
        offset += count
    return sibling


def per_device(section_updates, upper_rhs, pivot_inverse, coupling, extend_lists):
    leaves = lax.axis_size("leaf")
    fronts = lax.axis_size("front")
    levels = leaves.bit_length() - 1
    position = lax.axis_index("leaf")
    column = lax.axis_index("front")
    rhs_width = upper_rhs.shape[1]
    piv_dev = PIV // fronts
    upd_dev = UPD // fronts
    piv_blocks = piv_dev // BLK
    upd_blocks = upd_dev // BLK
    block_count = UPD // BLK
    local_blocks = jnp.concatenate(
        [
            column * piv_blocks + jnp.arange(piv_blocks, dtype=jnp.int32),
            PIV // BLK + column * upd_blocks + jnp.arange(upd_blocks, dtype=jnp.int32),
        ]
    )
    local_count = piv_blocks + upd_blocks
    carried = section_updates
    own_pieces = own_pieces_of(upper_rhs, levels, piv_dev)
    exchange_round(own_pieces, levels, position, 0)
    saved_part = []
    saved_half = []
    for height in range(1, levels + 1):
        group_size = 2**height
        span_rows = PIV // group_size
        band_start = PIV - PIV // 2 ** (height - 1)
        rhs_len = piv_dev // group_size
        rhs_start = piv_dev - piv_dev // 2 ** (height - 1)
        member = position & group_size - 1
        own_child = child_base(leaves, height) + (position >> height - 1)
        if height == 1:
            sibling = partner(carried, "leaf", height - 1)
        else:
            sibling = exchange_round(own_pieces, levels, position, height - 1, carried)
        pair_blocks = jnp.concatenate(
            [front_gather(carried[None]), front_gather(sibling[None])], 0
        )
        pair_lists = jnp.stack(
            [list_row(extend_lists, own_child), list_row(extend_lists, own_child ^ 1)]
        )[:, column ^ jnp.array(gathered_order(fronts), jnp.int32)]
        chooser = (pair_lists.reshape(2 * block_count)[None, :] == local_blocks[:, None]).astype(
            jnp.bfloat16
        )
        assembled = jnp.dot(
            chooser,
            pair_blocks.reshape(2 * block_count, BLK * rhs_width),
            preferred_element_type=jnp.float32,
        ).reshape(local_count * BLK, rhs_width)
        own_rows = own_pieces[height]
        rows_half = (own_rows + assembled[:piv_dev]).astype(jnp.bfloat16)
        g_share = pivot_inverse[band_start : band_start + span_rows]
        pivot_part = front_sum(
            jnp.dot(g_share, rows_half, preferred_element_type=jnp.float32)
        )
        pivot_half = pivot_part.astype(jnp.bfloat16)
        saved_part.append(pivot_part)
        saved_half.append(pivot_half)
        if height < levels:
            c_share = coupling[:, band_start : band_start + span_rows]
            summand = jnp.dot(c_share, pivot_half, preferred_element_type=jnp.float32)
            frame_upd = assembled[piv_dev:]
            carried = (frame_upd - sum_updates(summand, height)).astype(jnp.bfloat16)
    from_above = carried
    outputs = []
    for height in range(levels, 0, -1):
        group_size = 2**height
        span_rows = PIV // group_size
        band_start = PIV - PIV // 2 ** (height - 1)
        member = position & group_size - 1
        pivot_part = saved_part[height - 1]
        if height < levels:
            c_share = coupling[:, band_start : band_start + span_rows]
            back_total = front_sum(
                jnp.einsum("up,ur->pr", c_share, from_above, preferred_element_type=jnp.float32)
            )
            weight_half = (pivot_part - back_total).astype(jnp.bfloat16)
            upper_rows = from_above
        else:
            weight_half = saved_half[height - 1]
            upper_rows = jnp.zeros((upd_dev, rhs_width), jnp.bfloat16)
        g_share = pivot_inverse[band_start : band_start + span_rows]
        solve_term = jnp.einsum(
            "cp,cr->pr", g_share, weight_half, preferred_element_type=jnp.float32
        )
        part_len = piv_dev // group_size
        summed = sum_solution(solve_term, height)
        portion = lax.dynamic_slice_in_dim(summed, member * part_len, part_len, 0)
        rows_half = summed.astype(jnp.bfloat16)
        outputs.append(portion)
        frame_half = jnp.concatenate([rows_half, upper_rows], 0).reshape(
            local_count, BLK * rhs_width
        )
        child_list = list_row(extend_lists, child_base(leaves, height) + (position >> height - 1))
        picker = (child_list[:, None] == local_blocks[None, :]).astype(jnp.bfloat16)
        outgoing = (
            jnp.dot(picker, frame_half, preferred_element_type=jnp.float32)
            .astype(jnp.bfloat16)
            .reshape(fronts, upd_dev, rhs_width)
        )
        from_above = front_scatter_sum(outgoing)
    solution = jnp.concatenate(outputs[::-1], 0)
    return (solution, from_above)


def solution(mesh):
    placed = (
        P(("leaf", "front"), None),
        P(("leaf", "front"), None),
        P("leaf", "front"),
        P("front", "leaf"),
        P(),
    )
    return jax.shard_map(
        per_device,
        mesh=mesh,
        in_specs=placed,
        out_specs=(P(("leaf", "front"), None), P(("leaf", "front"), None)),
        check_vma=False,
    )
```

```python
import jax
import jax.numpy as jnp
from jax import lax
from jax.sharding import PartitionSpec as P

PIV = 4096
UPD = 1024
BLK = 128


def partner(block, axis, stride):
    count = lax.axis_size(axis)
    route = []
    for low in range(count):
        high = low | 1 << stride
        if high != low and high < count:
            route += [(low, high), (high, low)]
    return lax.ppermute(block, axis, route)


def child_base(leaves, height):
    total_rows = 0
    for depth in range(height - 1):
        total_rows = total_rows + leaves // 2**depth
    return total_rows


def list_row(extend_lists, row_index):
    return lax.dynamic_slice_in_dim(extend_lists, row_index, 1, 0)[0]


def upper_bit(position, bit_index):
    return position >> bit_index & 1 == 1


def joined(position, bit_index, portion, partner_rows):
    return jnp.where(
        upper_bit(position, bit_index),
        jnp.concatenate([partner_rows, portion], 0),
        jnp.concatenate([portion, partner_rows], 0),
    )


def gather_own(portion, height, position):
    for bit_index in range(height):
        partner_rows = partner(portion.astype(jnp.bfloat16), "leaf", bit_index).astype(
            portion.dtype
        )
        portion = joined(position, bit_index, portion, partner_rows)
    return portion


def sum_updates(summand, height):
    for bit_index in range(height):
        summand = summand + partner(summand.astype(jnp.bfloat16), "leaf", bit_index).astype(
            summand.dtype
        )
    return summand


def sum_solution(summand, height):
    for bit_index in range(height):
        summand = summand + partner(summand.astype(jnp.bfloat16), "leaf", bit_index).astype(
            summand.dtype
        )
    return summand


def front_sum(summand):
    bits = lax.axis_size("front").bit_length() - 1
    if summand.shape[0] < 512:
        for bit_index in range(bits):
            half = summand.astype(jnp.bfloat16)
            summand = half.astype(jnp.float32) + partner(half, "front", bit_index).astype(
                jnp.float32
            )
        return summand
    column = lax.axis_index("front")
    half_rows = summand.shape[0] // 2
    upper = column & 1
    keep = lax.dynamic_slice_in_dim(summand, upper * half_rows, half_rows, 0)
    send = lax.dynamic_slice_in_dim(summand, (1 - upper) * half_rows, half_rows, 0)
    summand = keep + partner(send.astype(jnp.bfloat16), "front", 0).astype(jnp.float32)
    for bit_index in range(1, bits):
        half = summand.astype(jnp.bfloat16)
        summand = half.astype(jnp.float32) + partner(half, "front", bit_index).astype(
            jnp.float32
        )
    summand = summand.astype(jnp.bfloat16)
    summand = joined(column, 0, summand, partner(summand, "front", 0))
    return summand.astype(jnp.float32)


def front_gather(blocks):
    bits = lax.axis_size("front").bit_length() - 1
    for bit_index in reversed(range(bits)):
        blocks = jnp.concatenate([blocks, partner(blocks, "front", bit_index)], 1)
    return blocks


def gathered_order(count):
    bits = count.bit_length() - 1
    return [int(format(index, f"0{bits}b")[::-1], 2) for index in range(count)]


def front_scatter_sum(outgoing):
    bits = lax.axis_size("front").bit_length() - 1
    column = lax.axis_index("front")
    rest = outgoing.shape[1:]
    split = outgoing.reshape((2,) * bits + rest)
    for bit_index in range(bits):
        axis = bits - 1 - bit_index
        mine = column >> bit_index & 1
        keep = lax.dynamic_index_in_dim(split, mine, axis, keepdims=False)
        send = lax.dynamic_index_in_dim(split, 1 - mine, axis, keepdims=False)
        received = partner(send, "front", bit_index)
        split = (keep.astype(jnp.float32) + received.astype(jnp.float32)).astype(outgoing.dtype)
    return split


def own_pieces_of(upper_rhs, levels, piv_dev):
    pieces = {}
    for height in range(1, levels + 1):
        rhs_len = piv_dev // 2**height
        rhs_start = piv_dev - piv_dev // 2 ** (height - 1)
        pieces[height] = upper_rhs[rhs_start : rhs_start + rhs_len]
    return pieces


def exchange_round(pieces, levels, position, bit_index, carried=None):
    active = [height for height in range(bit_index + 1, levels + 1)]
    parts = [pieces[height].astype(jnp.bfloat16) for height in active]
    if carried is not None:
        parts = [carried] + parts
    received = partner(jnp.concatenate(parts, 0), "leaf", bit_index)
    offset = 0
    sibling = None
    if carried is not None:
        sibling = received[: carried.shape[0]]
        offset = carried.shape[0]
    for height in active:
        count = pieces[height].shape[0]
        pieces[height] = joined(
            position,
            bit_index,
            pieces[height],
            received[offset : offset + count].astype(pieces[height].dtype),
        )
        offset += count
    return sibling


def sum_solution_halved(summand, height, position):
    half_rows = summand.shape[0] // 2
    upper = position & 1
    keep = lax.dynamic_slice_in_dim(summand, upper * half_rows, half_rows, 0)
    send = lax.dynamic_slice_in_dim(summand, (1 - upper) * half_rows, half_rows, 0)
    summand = keep + partner(send.astype(jnp.bfloat16), "leaf", 0).astype(summand.dtype)
    for bit_index in range(1, height):
        summand = summand + partner(summand.astype(jnp.bfloat16), "leaf", bit_index).astype(
            summand.dtype
        )
    received = partner(summand.astype(jnp.bfloat16), "leaf", 0).astype(summand.dtype)
    return joined(position, 0, summand, received)


def per_device(section_updates, upper_rhs, pivot_inverse, coupling, extend_lists):
    leaves = lax.axis_size("leaf")
    fronts = lax.axis_size("front")
    levels = leaves.bit_length() - 1
    position = lax.axis_index("leaf")
    column = lax.axis_index("front")
    rhs_width = upper_rhs.shape[1]
    piv_dev = PIV // fronts
    upd_dev = UPD // fronts
    piv_blocks = piv_dev // BLK
    upd_blocks = upd_dev // BLK
    block_count = UPD // BLK
    local_blocks = jnp.concatenate(
        [
            column * piv_blocks + jnp.arange(piv_blocks, dtype=jnp.int32),
            PIV // BLK + column * upd_blocks + jnp.arange(upd_blocks, dtype=jnp.int32),
        ]
    )
    local_count = piv_blocks + upd_blocks
    carried = section_updates
    own_pieces = own_pieces_of(upper_rhs, levels, piv_dev)
    exchange_round(own_pieces, levels, position, 0)
    saved_part = []
    saved_half = []
    for height in range(1, levels + 1):
        group_size = 2**height
        span_rows = PIV // group_size
        band_start = PIV - PIV // 2 ** (height - 1)
        rhs_len = piv_dev // group_size
        rhs_start = piv_dev - piv_dev // 2 ** (height - 1)
        member = position & group_size - 1
        own_child = child_base(leaves, height) + (position >> height - 1)
        if height == 1:
            sibling = partner(carried, "leaf", height - 1)
        else:
            sibling = exchange_round(own_pieces, levels, position, height - 1, carried)
        pair_blocks = jnp.concatenate(
            [front_gather(carried[None]), front_gather(sibling[None])], 0
        )
        pair_lists = jnp.stack(
            [list_row(extend_lists, own_child), list_row(extend_lists, own_child ^ 1)]
        )[:, column ^ jnp.array(gathered_order(fronts), jnp.int32)]
        chooser = (pair_lists.reshape(2 * block_count)[None, :] == local_blocks[:, None]).astype(
            jnp.bfloat16
        )
        assembled = jnp.dot(
            chooser,
            pair_blocks.reshape(2 * block_count, BLK * rhs_width),
            preferred_element_type=jnp.float32,
        ).reshape(local_count * BLK, rhs_width)
        own_rows = own_pieces[height]
        rows_half = (own_rows + assembled[:piv_dev]).astype(jnp.bfloat16)
        g_share = pivot_inverse[band_start : band_start + span_rows]
        pivot_part = front_sum(
            jnp.dot(g_share, rows_half, preferred_element_type=jnp.float32)
        )
        pivot_half = pivot_part.astype(jnp.bfloat16)
        saved_part.append(pivot_part)
        saved_half.append(pivot_half)
        if height < levels:
            c_share = coupling[:, band_start : band_start + span_rows]
            summand = jnp.dot(c_share, pivot_half, preferred_element_type=jnp.float32)
            frame_upd = assembled[piv_dev:]
            carried = (frame_upd - sum_updates(summand, height)).astype(jnp.bfloat16)
    from_above = carried
    outputs = []
    for height in range(levels, 0, -1):
        group_size = 2**height
        span_rows = PIV // group_size
        band_start = PIV - PIV // 2 ** (height - 1)
        member = position & group_size - 1
        pivot_part = saved_part[height - 1]
        if height < levels:
            c_share = coupling[:, band_start : band_start + span_rows]
            back_total = front_sum(
                jnp.einsum("up,ur->pr", c_share, from_above, preferred_element_type=jnp.float32)
            )
            weight_half = (pivot_part - back_total).astype(jnp.bfloat16)
            upper_rows = from_above
        else:
            weight_half = saved_half[height - 1]
            upper_rows = jnp.zeros((upd_dev, rhs_width), jnp.bfloat16)
        g_share = pivot_inverse[band_start : band_start + span_rows]
        solve_term = jnp.einsum(
            "cp,cr->pr", g_share, weight_half, preferred_element_type=jnp.float32
        )
        part_len = piv_dev // group_size
        if height == levels:
            summed = sum_solution_halved(solve_term, height, position)
        else:
            summed = sum_solution(solve_term, height)
        portion = lax.dynamic_slice_in_dim(summed, member * part_len, part_len, 0)
        rows_half = summed.astype(jnp.bfloat16)
        outputs.append(portion)
        frame_half = jnp.concatenate([rows_half, upper_rows], 0).reshape(
            local_count, BLK * rhs_width
        )
        child_list = list_row(extend_lists, child_base(leaves, height) + (position >> height - 1))
        picker = (child_list[:, None] == local_blocks[None, :]).astype(jnp.bfloat16)
        outgoing = (
            jnp.dot(picker, frame_half, preferred_element_type=jnp.float32)
            .astype(jnp.bfloat16)
            .reshape(fronts, upd_dev, rhs_width)
        )
        from_above = front_scatter_sum(outgoing)
    solution = jnp.concatenate(outputs[::-1], 0)
    return (solution, from_above)


def solution(mesh):
    placed = (
        P(("leaf", "front"), None),
        P(("leaf", "front"), None),
        P("leaf", "front"),
        P("front", "leaf"),
        P(),
    )
    return jax.shard_map(
        per_device,
        mesh=mesh,
        in_specs=placed,
        out_specs=(P(("leaf", "front"), None), P(("leaf", "front"), None)),
        check_vma=False,
    )
```

```python
import jax
import jax.numpy as jnp
from jax import lax
from jax.sharding import PartitionSpec as P

PIV = 4096
UPD = 1024
BLK = 128


def partner(block, axis, stride):
    count = lax.axis_size(axis)
    route = []
    for low in range(count):
        high = low | 1 << stride
        if high != low and high < count:
            route += [(low, high), (high, low)]
    return lax.ppermute(block, axis, route)


def child_base(leaves, height):
    total_rows = 0
    for depth in range(height - 1):
        total_rows = total_rows + leaves // 2**depth
    return total_rows


def list_row(extend_lists, row_index):
    return lax.dynamic_slice_in_dim(extend_lists, row_index, 1, 0)[0]


def upper_bit(position, bit_index):
    return position >> bit_index & 1 == 1


def joined(position, bit_index, portion, partner_rows):
    return jnp.where(
        upper_bit(position, bit_index),
        jnp.concatenate([partner_rows, portion], 0),
        jnp.concatenate([portion, partner_rows], 0),
    )


def gather_own(portion, height, position):
    for bit_index in range(height):
        partner_rows = partner(portion.astype(jnp.bfloat16), "leaf", bit_index).astype(
            portion.dtype
        )
        portion = joined(position, bit_index, portion, partner_rows)
    return portion


def sum_updates(summand, height):
    for bit_index in range(height):
        summand = summand + partner(summand.astype(jnp.bfloat16), "leaf", bit_index).astype(
            summand.dtype
        )
    return summand


def sum_solution(summand, height):
    for bit_index in range(height):
        summand = summand + partner(summand.astype(jnp.bfloat16), "leaf", bit_index).astype(
            summand.dtype
        )
    return summand


def front_sum(summand):
    bits = lax.axis_size("front").bit_length() - 1
    if summand.shape[0] < 512:
        for bit_index in range(bits):
            half = summand.astype(jnp.bfloat16)
            summand = half.astype(jnp.float32) + partner(half, "front", bit_index).astype(
                jnp.float32
            )
        return summand
    column = lax.axis_index("front")
    half_rows = summand.shape[0] // 2
    upper = column & 1
    keep = lax.dynamic_slice_in_dim(summand, upper * half_rows, half_rows, 0)
    send = lax.dynamic_slice_in_dim(summand, (1 - upper) * half_rows, half_rows, 0)
    summand = keep + partner(send.astype(jnp.bfloat16), "front", 0).astype(jnp.float32)
    for bit_index in range(1, bits):
        half = summand.astype(jnp.bfloat16)
        summand = half.astype(jnp.float32) + partner(half, "front", bit_index).astype(
            jnp.float32
        )
    summand = summand.astype(jnp.bfloat16)
    summand = joined(column, 0, summand, partner(summand, "front", 0))
    return summand.astype(jnp.float32)


def front_gather(blocks):
    bits = lax.axis_size("front").bit_length() - 1
    for bit_index in reversed(range(bits)):
        blocks = jnp.concatenate([blocks, partner(blocks, "front", bit_index)], 1)
    return blocks


def gathered_order(count):
    bits = count.bit_length() - 1
    return [int(format(index, f"0{bits}b")[::-1], 2) for index in range(count)]


def front_scatter_sum(outgoing):
    bits = lax.axis_size("front").bit_length() - 1
    column = lax.axis_index("front")
    rest = outgoing.shape[1:]
    split = outgoing.reshape((2,) * bits + rest)
    for bit_index in range(bits):
        axis = bits - 1 - bit_index
        mine = column >> bit_index & 1
        keep = lax.dynamic_index_in_dim(split, mine, axis, keepdims=False)
        send = lax.dynamic_index_in_dim(split, 1 - mine, axis, keepdims=False)
        received = partner(send, "front", bit_index)
        split = (keep.astype(jnp.float32) + received.astype(jnp.float32)).astype(outgoing.dtype)
    return split


def own_pieces_of(upper_rhs, levels, piv_dev):
    pieces = {}
    for height in range(1, levels + 1):
        rhs_len = piv_dev // 2**height
        rhs_start = piv_dev - piv_dev // 2 ** (height - 1)
        pieces[height] = upper_rhs[rhs_start : rhs_start + rhs_len]
    return pieces


def exchange_round(pieces, levels, position, bit_index, carried=None):
    active = [height for height in range(bit_index + 1, levels + 1)]
    parts = [pieces[height].astype(jnp.bfloat16) for height in active]
    if carried is not None:
        parts = [carried] + parts
    received = partner(jnp.concatenate(parts, 0), "leaf", bit_index)
    offset = 0
    sibling = None
    if carried is not None:
        sibling = received[: carried.shape[0]]
        offset = carried.shape[0]
    for height in active:
        count = pieces[height].shape[0]
        pieces[height] = joined(
            position,
            bit_index,
            pieces[height],
            received[offset : offset + count].astype(pieces[height].dtype),
        )
        offset += count
    return sibling


def sum_solution_halved(summand, height, position):
    half_rows = summand.shape[0] // 2
    upper = position & 1
    keep = lax.dynamic_slice_in_dim(summand, upper * half_rows, half_rows, 0)
    send = lax.dynamic_slice_in_dim(summand, (1 - upper) * half_rows, half_rows, 0)
    summand = keep + partner(send.astype(jnp.bfloat16), "leaf", 0).astype(summand.dtype)
    for bit_index in range(1, height):
        summand = summand + partner(summand.astype(jnp.bfloat16), "leaf", bit_index).astype(
            summand.dtype
        )
    received = partner(summand.astype(jnp.bfloat16), "leaf", 0).astype(summand.dtype)
    return joined(position, 0, summand, received)


def per_device(section_updates, upper_rhs, pivot_inverse, coupling, extend_lists):
    leaves = lax.axis_size("leaf")
    fronts = lax.axis_size("front")
    levels = leaves.bit_length() - 1
    position = lax.axis_index("leaf")
    column = lax.axis_index("front")
    rhs_width = upper_rhs.shape[1]
    piv_dev = PIV // fronts
    upd_dev = UPD // fronts
    piv_blocks = piv_dev // BLK
    upd_blocks = upd_dev // BLK
    block_count = UPD // BLK
    local_blocks = jnp.concatenate(
        [
            column * piv_blocks + jnp.arange(piv_blocks, dtype=jnp.int32),
            PIV // BLK + column * upd_blocks + jnp.arange(upd_blocks, dtype=jnp.int32),
        ]
    )
    local_count = piv_blocks + upd_blocks
    carried = section_updates
    own_pieces = own_pieces_of(upper_rhs, levels, piv_dev)
    exchange_round(own_pieces, levels, position, 0)
    saved_part = []
    saved_half = []
    for height in range(1, levels + 1):
        group_size = 2**height
        span_rows = PIV // group_size
        band_start = PIV - PIV // 2 ** (height - 1)
        rhs_len = piv_dev // group_size
        rhs_start = piv_dev - piv_dev // 2 ** (height - 1)
        member = position & group_size - 1
        own_child = child_base(leaves, height) + (position >> height - 1)
        if height == 1:
            sibling = partner(carried, "leaf", height - 1)
        else:
            sibling = exchange_round(own_pieces, levels, position, height - 1, carried)
        pair_blocks = jnp.concatenate(
            [front_gather(carried[None]), front_gather(sibling[None])], 0
        )
        pair_lists = jnp.stack(
            [list_row(extend_lists, own_child), list_row(extend_lists, own_child ^ 1)]
        )[:, column ^ jnp.array(gathered_order(fronts), jnp.int32)]
        chooser = (pair_lists.reshape(2 * block_count)[None, :] == local_blocks[:, None]).astype(
            jnp.bfloat16
        )
        assembled = jnp.dot(
            chooser,
            pair_blocks.reshape(2 * block_count, BLK * rhs_width),
            preferred_element_type=jnp.float32,
        ).reshape(local_count * BLK, rhs_width)
        own_rows = own_pieces[height]
        rows_half = (own_rows + assembled[:piv_dev]).astype(jnp.bfloat16)
        g_share = pivot_inverse[band_start : band_start + span_rows]
        pivot_part = front_sum(
            jnp.dot(g_share, rows_half, preferred_element_type=jnp.float32)
        )
        pivot_half = pivot_part.astype(jnp.bfloat16)
        saved_part.append(pivot_part)
        saved_half.append(pivot_half)
        if height < levels:
            c_share = coupling[:, band_start : band_start + span_rows]
            summand = jnp.dot(c_share, pivot_half, preferred_element_type=jnp.float32)
            frame_upd = assembled[piv_dev:]
            carried = (frame_upd - sum_updates(summand, height)).astype(jnp.bfloat16)
    from_above = carried
    outputs = []
    for height in range(levels, 0, -1):
        group_size = 2**height
        span_rows = PIV // group_size
        band_start = PIV - PIV // 2 ** (height - 1)
        member = position & group_size - 1
        pivot_part = saved_part[height - 1]
        if height < levels:
            c_share = coupling[:, band_start : band_start + span_rows]
            back_total = front_sum(
                jnp.einsum("up,ur->pr", c_share, from_above, preferred_element_type=jnp.float32)
            )
            weight_half = (pivot_part - back_total).astype(jnp.bfloat16)
            upper_rows = from_above
        else:
            weight_half = saved_half[height - 1]
            upper_rows = jnp.zeros((upd_dev, rhs_width), jnp.bfloat16)
        g_share = pivot_inverse[band_start : band_start + span_rows]
        solve_term = jnp.einsum(
            "cp,cr->pr", g_share, weight_half, preferred_element_type=jnp.float32
        )
        part_len = piv_dev // group_size
        if height >= levels - 1:
            summed = sum_solution_halved(solve_term, height, position)
        else:
            summed = sum_solution(solve_term, height)
        portion = lax.dynamic_slice_in_dim(summed, member * part_len, part_len, 0)
        rows_half = summed.astype(jnp.bfloat16)
        outputs.append(portion)
        frame_half = jnp.concatenate([rows_half, upper_rows], 0).reshape(
            local_count, BLK * rhs_width
        )
        child_list = list_row(extend_lists, child_base(leaves, height) + (position >> height - 1))
        picker = (child_list[:, None] == local_blocks[None, :]).astype(jnp.bfloat16)
        outgoing = (
            jnp.dot(picker, frame_half, preferred_element_type=jnp.float32)
            .astype(jnp.bfloat16)
            .reshape(fronts, upd_dev, rhs_width)
        )
        from_above = front_scatter_sum(outgoing)
    solution = jnp.concatenate(outputs[::-1], 0)
    return (solution, from_above)


def solution(mesh):
    placed = (
        P(("leaf", "front"), None),
        P(("leaf", "front"), None),
        P("leaf", "front"),
        P("front", "leaf"),
        P(),
    )
    return jax.shard_map(
        per_device,
        mesh=mesh,
        in_specs=placed,
        out_specs=(P(("leaf", "front"), None), P(("leaf", "front"), None)),
        check_vma=False,
    )
```
